32 devices in a mesh: row: 4 (over y, x), seq: 2 (over core), head: 4 (over z).
Axes of the slice: x: 2, y: 2, z: 4, core: 2. Of those that a mesh axis runs over, the one named last changes fastest.
Arguments:
- inputs: bfloat16 [16, 1024, 768], P('row', ('seq', 'head')), may hold values from -6 to 6
- segment_ids: int32 [16, 1024], P('row', 'seq'), may hold values from 0 to 63, as said below
- w_project: bfloat16 [12, 3, 64, 768], P('head'), may hold values from -0.375 to 0.375
- proj_bias: bfloat16 [2, 768], P(None, 'head'), may hold values from -3 to 3
- conv_taps: bfloat16 [12, 33], P('head'), may hold values from -0.375 to 0.375
- w_output: bfloat16 [768, 768], P('head'), may hold values from -0.375 to 0.375
- out_bias: bfloat16 [768], replicated, may hold values from -1.75 to 1.75
- norm_attn: bfloat16 [2, 768], replicated, may hold values from 0.25 to 1.75
- w_hidden: bfloat16 [768, 3072], P(None, 'head'), may hold values from -0.21875 to 0.21875
- hid_bias: bfloat16 [3072], P('head'), may hold values from -3 to 3
- w_down: bfloat16 [3072, 768], P('head'), may hold values from -0.15625 to 0.15625
- down_bias: bfloat16 [768], replicated, may hold values from -1.75 to 1.75
- norm_ffn: bfloat16 [2, 768], replicated, may hold values from 0.25 to 1.75
- cotangent: bfloat16 [16, 1024, 768], P('row', ('seq', 'head')), may hold values from -6 to 6
Outputs:
- layer_out: bfloat16 [16, 1024, 768], P('row', ('seq', 'head'))
- grad_inputs: bfloat16 [16, 1024, 768], P('row', ('seq', 'head'))
- grad_project: float32 [12, 3, 64, 768], P('head', None, None, ('row', 'seq'))
- grad_projbias: float32 [2, 768], P(None, 'head')
- grad_conv: float32 [12, 33], P('head')
- grad_output: float32 [768, 768], P('head', ('row', 'seq'))
- grad_outbias: float32 [768], P('head')
- grad_normattn: float32 [2, 768], P(None, 'head')
- grad_hidden: float32 [768, 3072], P(('row', 'seq'), 'head')
- grad_hidbias: float32 [3072], P('head')
- grad_down: float32 [3072, 768], P('head', ('row', 'seq'))
- grad_downbias: float32 [768], P('head')
- grad_normffn: float32 [2, 768], P(None, 'head')
The draws below stay inside these ranges and needn't reach their ends.
Inputs may be any that keep to these rules, and one draw needn't show every extreme that they name: `segment_ids`: along each document the ids never fall; every id occurs, on 1 to 31 consecutive positions, both extremes reached in every document; segment i ends fewer than 16 positions after position (i + 1) * 16.
All inputs are finite; a program needn't handle non-finite values.
Results may differ from the reference program's by a relative error of at most 0.024.
The reference program's roundings to bfloat16 on the way count: a program that leaves them out, or rounds other values in their place, can miss the bound.
Values may be sent and summed in bfloat16 or wider, within the bound.
A program may use at most 192 MiB of HBM per device.

```python
import jax
import jax.numpy as jnp
from jax import lax

D = 768
HEADS = 12
HEAD_DIM = 64
FF = 3072
LANDMARKS = 64
CONV_TAPS = 33
NEWTON_STEPS = 6
LENGTH = 1024
BATCH = 16


def segment_layout(key):
    stride_len = LENGTH // LANDMARKS
    key_move, key_pick = jax.random.split(key)
    shifts = jax.random.randint(key_move, (BATCH, LANDMARKS), 0, stride_len)
    chosen = jax.random.randint(key_pick, (BATCH, 1), 1, LANDMARKS - 2)
    column = jnp.arange(LANDMARKS)[None, :]
    shifts = jnp.where(column == chosen, stride_len - 1, shifts)
    cleared = (column == chosen - 1) | (column == chosen + 1) | (column == LANDMARKS - 1)
    shifts = jnp.where(cleared, 0, shifts)
    bounds = (column + 1) * stride_len + shifts
    position = jnp.arange(LENGTH)[None, :, None]
    return jnp.sum((position >= bounds[:, None, :]).astype(jnp.int32), axis=-1)


def draw_segment_ids(key, part):
    return segment_layout(jax.random.fold_in(key, 11))


def draw_inputs(key, part):
    segments = segment_layout(jax.random.fold_in(key, 11))
    key_common, key_noise = jax.random.split(jax.random.fold_in(key, 23), 2)
    common = jax.random.normal(key_common, (BATCH, LANDMARKS, D), jnp.float32)
    spread = common[jnp.arange(BATCH)[:, None], segments]
    noise = jax.random.normal(key_noise, (BATCH, LENGTH, D), jnp.float32)
    values = 0.7 * spread + 0.7 * noise
    return jnp.clip(values, -6.0, 6.0).astype(jnp.bfloat16)


def block_scale(rng, extent, pieces, smallest, high):
    gain = 1.0
    for dim, blocks in pieces:
        steps = jax.random.uniform(jax.random.fold_in(jax.random.fold_in(rng, 6), dim), (blocks,), jnp.float32, smallest / len(pieces), high / len(pieces))
        gain = gain * jnp.repeat(jnp.exp(steps), extent[dim] // blocks).reshape((-1,) + (1,) * (len(extent) - 1 - dim))
    return gain


def bell_draw(stream_key, shape, deviation, most, cuts=(), kind=jnp.bfloat16):
    drawn = jax.random.normal(stream_key, shape, jnp.float32) * deviation
    if len(cuts) > 0:
        drawn = block_scale(stream_key, shape, cuts, -0.22, 0.18) * drawn
    return jnp.clip(drawn, min=-most, max=most).astype(kind)


def setup_inputs(seed: int = 0) -> dict:
    arg_keys = jax.random.split(jax.random.key(seed), 15)
    return {
        "inputs": draw_inputs(jax.random.fold_in(arg_keys[14], 71), 0),
        "segment_ids": draw_segment_ids(jax.random.fold_in(arg_keys[14], 71), 0),
        "w_project": bell_draw(arg_keys[2], (HEADS, 3, HEAD_DIM, D), (D // 3) ** -0.5, 0.375, ((0, 4),)),
        "proj_bias": bell_draw(arg_keys[3], (2, D), 0.5, 3.0, ((1, 4),)),
        "conv_taps": bell_draw(arg_keys[4], (HEADS, CONV_TAPS), 0.06, 0.375, ((0, 4),)),
        "w_output": bell_draw(arg_keys[5], (D, D), (D // 3) ** -0.5, 0.375, ((0, 4),)),
        "out_bias": bell_draw(arg_keys[6], (D,), 0.3, 1.75),
        "norm_attn": jnp.clip(1.0 + 0.15 * jax.random.normal(arg_keys[7], (2, D), jnp.float32), 0.25, 1.75).astype(jnp.bfloat16),
        "w_hidden": bell_draw(arg_keys[8], (D, FF), D ** -0.5, 0.21875, ((1, 4),)),
        "hid_bias": bell_draw(arg_keys[9], (FF,), 0.5, 3.0, ((0, 4),)),
        "w_down": bell_draw(arg_keys[10], (FF, D), (FF // 2) ** -0.5, 0.15625, ((0, 4),)),
        "down_bias": bell_draw(arg_keys[11], (D,), 0.3, 1.75),
        "norm_ffn": jnp.clip(1.0 + 0.15 * jax.random.normal(arg_keys[12], (2, D), jnp.float32), 0.25, 1.75).astype(jnp.bfloat16),
        "cotangent": bell_draw(arg_keys[13], (BATCH, LENGTH, D), 1.0, 6.0, ((0, 4), (1, 8))),
    }


EPS = 1e-05
HIGH_ACCURACY = lax.Precision.HIGHEST

@jax.custom_vjp
def reduced_input(v):
    return lax.optimization_barrier(v.astype(jnp.bfloat16)).astype(jnp.float32)

@jax.custom_vjp
def reduced_backward(v):
    return v

def low_keep(v):
    return (reduced_input(v), None)

def low_pass(kept, grad):
    return (grad,)

def back_keep(v):
    return (v, None)

def back_low(kept, grad):
    return (reduced_input(grad),)
reduced_input.defvjp(low_keep, low_pass)
reduced_backward.defvjp(back_keep, back_low)

def newton_schulz_inverse(kernel):
    order_size = kernel.shape[-1]
    identity = jnp.eye(order_size, dtype=kernel.dtype)
    estimate = jnp.swapaxes(kernel, -1, -2) / order_size
    for repeat in range(NEWTON_STEPS):
        product = jnp.einsum('hij,hjk->hik', kernel, estimate, precision=HIGH_ACCURACY)
        nested = 7.0 * identity - product
        nested = 15.0 * identity - jnp.einsum('hij,hjk->hik', product, nested, precision=HIGH_ACCURACY)
        nested = 13.0 * identity - jnp.einsum('hij,hjk->hik', product, nested, precision=HIGH_ACCURACY)
        estimate = 0.25 * jnp.einsum('hij,hjk->hik', estimate, nested, precision=HIGH_ACCURACY)
    return estimate

def layer_norm(residual, params):
    center = residual - lax.optimization_barrier(jnp.mean(residual, axis=-1, keepdims=True))
    variance = lax.optimization_barrier(jnp.mean(center * center, axis=-1, keepdims=True))
    return center * lax.rsqrt(variance + EPS) * params[0] + params[1]

def layer(tokens, segments, w_project, proj_bias, conv_taps, w_output, out_bias, norm_attn, w_hidden, hid_bias, w_down, down_bias, norm_ffn):
    length = tokens.shape[0]
    half_taps = CONV_TAPS // 2
    scores_factor = HEAD_DIM ** (-0.5)
    mixed_proj = jnp.einsum('le,hcfe->clhf', tokens, w_project, precision=HIGH_ACCURACY).reshape(3, length, D)
    query_tokens = reduced_backward(reduced_input(mixed_proj[0] + proj_bias[0])).reshape(length, HEADS, HEAD_DIM)
    key_tokens = reduced_backward(reduced_input(mixed_proj[1])).reshape(length, HEADS, HEAD_DIM)
    value_tokens = reduced_backward(reduced_input(mixed_proj[2] + proj_bias[1])).reshape(length, HEADS, HEAD_DIM)
    segment_membership = (segments[:, None] == jnp.arange(LANDMARKS, dtype=jnp.int32)[None, :]).astype(tokens.dtype)
    segment_count = lax.optimization_barrier(jnp.sum(segment_membership, axis=0))
    query_landmarks = reduced_input(jnp.einsum('ep,erb->prb', segment_membership, query_tokens, precision=HIGH_ACCURACY) / segment_count[:, None, None])
    key_landmarks = reduced_input(jnp.einsum('ep,erb->prb', segment_membership, key_tokens, precision=HIGH_ACCURACY) / segment_count[:, None, None])
    first_scores = reduced_backward(jnp.einsum('fyg,iyg->yfi', query_tokens, key_landmarks, precision=HIGH_ACCURACY) * scores_factor)
    first_kernel = reduced_input(jax.nn.softmax(first_scores, axis=-1))
    second_kernel = jax.nn.softmax(jnp.einsum('ojz,kjz->jok', query_landmarks, key_landmarks, precision=HIGH_ACCURACY) * scores_factor, axis=-1)
    third_scores = reduced_backward(jnp.einsum('ceo,teo->ect', query_landmarks, key_tokens, precision=HIGH_ACCURACY) * scores_factor)
    third_kernel = jax.nn.softmax(third_scores, axis=-1)
    segment_means = jnp.einsum('pzt,tpi->pzi', third_kernel, value_tokens, precision=HIGH_ACCURACY)
    reduced_mixer = reduced_input(jnp.einsum('ogq,oqk->ogk', newton_schulz_inverse(second_kernel), segment_means, precision=HIGH_ACCURACY))
    landmark_output = jnp.einsum('fje,feu->jfu', first_kernel, reduced_mixer, precision=HIGH_ACCURACY)
    padded = jnp.pad(value_tokens, ((half_taps, half_taps), (0, 0), (0, 0)))
    conv_out = jnp.zeros_like(value_tokens)
    for offset in range(CONV_TAPS):
        conv_out = conv_out + conv_taps[:, offset][None, :, None] * padded[offset:offset + length]
    attended = reduced_backward(reduced_input((landmark_output + conv_out).reshape(length, D)))
    projected = reduced_backward(jnp.dot(attended, w_output, precision=HIGH_ACCURACY, preferred_element_type=jnp.float32) + out_bias)
    normed_one = layer_norm(tokens + projected, norm_attn)
    hidden_pre = reduced_backward(jnp.dot(reduced_input(normed_one), w_hidden, precision=HIGH_ACCURACY, preferred_element_type=jnp.float32) + hid_bias)
    active = reduced_input(jax.nn.gelu(hidden_pre, approximate=False))
    down_out = reduced_backward(jnp.dot(active, w_down, precision=HIGH_ACCURACY, preferred_element_type=jnp.float32) + down_bias)
    return layer_norm(normed_one + down_out, norm_ffn)

def reference(inputs, segment_ids, w_project, proj_bias, conv_taps, w_output, out_bias, norm_attn, w_hidden, hid_bias, w_down, down_bias, norm_ffn, cotangent):
    weights = tuple((weight_arg.astype(jnp.float32) for weight_arg in (w_project, proj_bias, conv_taps, w_output, out_bias, norm_attn, w_hidden, hid_bias, w_down, down_bias, norm_ffn)))

    def per_sequence(running, sliced):
        tokens, segments, upstream = sliced

        def forward(tokens_in, *weight_list):
            return layer(tokens_in, segments, *weight_list)
        layer_value, pullback = jax.vjp(forward, tokens.astype(jnp.float32), *weights)
        gradients = pullback(upstream.astype(jnp.float32))
        running = tuple((summed + grad_one for summed, grad_one in zip(running, gradients[1:])))
        return (running, (layer_value.astype(jnp.bfloat16), gradients[0].astype(jnp.bfloat16)))
    zeros_init = tuple((jnp.zeros_like(weight_arg) for weight_arg in weights))
    totals, outputs = lax.scan(per_sequence, zeros_init, (inputs, segment_ids, cotangent))
    return (outputs[0], outputs[1], totals[0], totals[1], totals[2], totals[3], totals[4], totals[5], totals[6], totals[7], totals[8], totals[9], totals[10])
```

```python
import jax
import jax.numpy as jnp
from jax import lax
from jax.sharding import PartitionSpec as P

HEAD_DIM = 64
LANDMARKS = 64
CONV_TAPS = 33
NEWTON_STEPS = 6


EPS = 1e-05
HIGH_ACCURACY = lax.Precision.HIGHEST


def combined_all(part, axis, combine):
    gathered = jax.tree.map(lambda a: lax.all_gather(a, axis), part)

    def take(source):
        return jax.tree.map(lambda a: lax.dynamic_index_in_dim(a, source, 0, False), gathered)

    return lax.fori_loop(
        1, lax.axis_size(axis), lambda source, state: combine(state, take(source)), take(0)
    )


def padded(cells, sides, width):
    for axis, dim in sides:
        count = lax.axis_size(axis)
        ends = count - 1
        head = lax.slice_in_dim(cells, 0, width, axis=dim)
        tail = lax.slice_in_dim(cells, cells.shape[dim] - width, cells.shape[dim], axis=dim)
        cells = jnp.concatenate(
            [
                lax.ppermute(tail, axis, [(i, (i + 1) % count) for i in range(ends)]),
                cells,
                lax.ppermute(head, axis, [((i + 1) % count, i) for i in range(ends)]),
            ],
            axis=dim,
        )
    return cells


def newton_schulz_inverse(kernel):
    order_size = kernel.shape[-1]
    identity = jnp.eye(order_size, dtype=jnp.float32)
    estimate = jnp.swapaxes(kernel, -1, -2) / order_size
    for repeat in range(NEWTON_STEPS):
        product = jnp.einsum("...ij,...jk->...ik", kernel, estimate, precision=HIGH_ACCURACY)
        nested = 7.0 * identity - product
        nested = 15.0 * identity - jnp.einsum(
            "...ij,...jk->...ik", product, nested, precision=HIGH_ACCURACY
        )
        nested = 13.0 * identity - jnp.einsum(
            "...ij,...jk->...ik", product, nested, precision=HIGH_ACCURACY
        )
        estimate = 0.25 * jnp.einsum(
            "...ij,...jk->...ik", estimate, nested, precision=HIGH_ACCURACY
        )
    return estimate


def exact_gelu(pre_act):
    return jax.nn.gelu(pre_act, approximate=False)


def merge_softmax(former, latter):
    top_one, total_one, pooled_one = former
    top_two, total_two, pooled_two = latter
    top_new = jnp.maximum(top_one, top_two)
    factor_one = jnp.exp(top_one - top_new)
    factor_two = jnp.exp(top_two - top_new)
    return (
        top_new,
        total_one * factor_one + total_two * factor_two,
        pooled_one * factor_one[..., None] + pooled_two * factor_two[..., None],
    )


def swap_sum(tree):
    if lax.axis_size("seq") == 2:
        other = jax.tree.map(lambda a: lax.ppermute(a, "seq", [(0, 1), (1, 0)]), tree)
        return jax.tree.map(lambda a, b: a + b, tree, other)
    return lax.psum(tree, "seq")


def swap_merge(part, combine):
    if lax.axis_size("seq") == 2:
        other = jax.tree.map(lambda a: lax.ppermute(a, "seq", [(0, 1), (1, 0)]), part)
        return combine(part, other)
    return combined_all(part, "seq", combine)


def to_documents(rows):
    return lax.all_to_all(rows, "head", split_axis=0, concat_axis=1, tiled=True)


def to_positions(rows):
    return lax.all_to_all(rows, "head", split_axis=1, concat_axis=0, tiled=True)


ALL_AXES = ("head", "row", "seq")


def gather_weight(shard):
    count = lax.axis_size("row") * lax.axis_size("seq")
    place = lax.axis_index("row") * lax.axis_size("seq") + lax.axis_index("seq")
    size = shard.shape[0] // count
    piece = lax.dynamic_slice_in_dim(shard, place * size, size, axis=0)
    return lax.all_gather(piece, ALL_AXES, axis=0, tiled=True)


def scatter_grad(grad):
    shards, features, columns = grad.shape
    low = grad.reshape(shards * features, columns).astype(jnp.bfloat16)
    return lax.psum_scatter(low, ALL_AXES, scatter_dimension=0, tiled=True).astype(jnp.float32)


def norm_apply(residual, gain_row, shift_row):
    former = jnp.mean(residual, axis=-1)
    centered_raw = residual - former[..., None]
    variance = jnp.mean(centered_raw * centered_raw, axis=-1)
    inv_dev = lax.rsqrt(variance + EPS)
    centered = centered_raw * inv_dev[..., None]
    return (centered * gain_row + shift_row, centered, inv_dev)


def norm_back(incoming, centered, inv_dev, gain_row):
    scaled = incoming * gain_row
    former = jnp.mean(scaled, axis=-1)
    latter = jnp.mean(scaled * centered, axis=-1)
    return inv_dev[..., None] * (scaled - former[..., None] - centered * latter[..., None])


def norm_grads(incoming, centered):
    return jnp.stack([jnp.sum(incoming * centered, axis=(0, 1)), jnp.sum(incoming, axis=(0, 1))])


def on_device(
    inputs,
    segment_ids,
    w_project,
    proj_bias,
    conv_taps,
    w_output,
    out_bias,
    norm_attn,
    w_hidden,
    hid_bias,
    w_down,
    down_bias,
    norm_ffn,
    cotangent,
):
    model_width = inputs.shape[2]
    shards = lax.axis_size("head")
    heads_shard = w_project.shape[0]
    heads = heads_shard * shards
    hidden_shard = w_hidden.shape[1]
    width_shard = heads_shard * HEAD_DIM
    half_taps = CONV_TAPS // 2
    scores_factor = HEAD_DIM ** (-0.5)
    head_place = lax.axis_index("head")

    x_rows = to_documents(inputs)
    seqs, tokens, _ = x_rows.shape
    small_pack = jnp.concatenate([proj_bias.reshape(-1), conv_taps.reshape(-1), hid_bias])
    small_all = lax.all_gather(small_pack, "head", axis=0)
    split_one = 2 * width_shard
    split_two = split_one + heads_shard * CONV_TAPS
    bias_all = small_all[:, :split_one].reshape(shards, 2, width_shard)
    bias_all = jnp.swapaxes(bias_all, 0, 1).reshape(2, model_width)
    taps_all = small_all[:, split_one:split_two].reshape(heads, CONV_TAPS)
    hid_all = small_all[:, split_two:].reshape(shards * hidden_shard)

    proj_full = gather_weight(w_project.reshape(-1, model_width)).reshape(
        heads, 3, HEAD_DIM, model_width
    )
    out_full = gather_weight(w_output)
    hidden_full = gather_weight(w_hidden).reshape(shards, model_width, hidden_shard)
    down_full = gather_weight(w_down)
    grad_rows = to_documents(cotangent)

    segment_rows = lax.dynamic_slice_in_dim(segment_ids, head_place * seqs, seqs, axis=0)

    def split_heads(source, row_count):
        return source.reshape(seqs, row_count, heads, HEAD_DIM)

    mixed_proj = jnp.einsum(
        "ste,hcfe->csthf", x_rows, proj_full, preferred_element_type=jnp.float32
    )
    mixed_proj = mixed_proj.reshape(3, seqs, tokens, model_width)
    query_tokens = (mixed_proj[0] + bias_all[0]).astype(jnp.bfloat16)
    key_tokens = mixed_proj[1].astype(jnp.bfloat16)
    value_tokens = (mixed_proj[2] + bias_all[1]).astype(jnp.bfloat16)
    segment_membership = (
        segment_rows[:, :, None] == jnp.arange(LANDMARKS, dtype=jnp.int32)[None, None, :]
    )
    member_low = segment_membership.astype(jnp.bfloat16)
    member_wide = segment_membership.astype(jnp.float32)
    query_sums = jnp.einsum(
        "stm,std->smd", member_low, query_tokens, preferred_element_type=jnp.float32
    )
    key_sums = jnp.einsum(
        "stm,std->smd", member_low, key_tokens, preferred_element_type=jnp.float32
    )
    segment_count = jnp.sum(member_wide, axis=1)
    query_sums, key_sums, segment_count = swap_sum((query_sums, key_sums, segment_count))
    query_landmarks = (query_sums / segment_count[:, :, None]).astype(jnp.bfloat16)
    key_landmarks = (key_sums / segment_count[:, :, None]).astype(jnp.bfloat16)
    q_heads = split_heads(query_tokens, tokens)
    k_heads = split_heads(key_tokens, tokens)
    v_heads = split_heads(value_tokens, tokens)
    ql_heads = split_heads(query_landmarks, LANDMARKS)
    kl_heads = split_heads(key_landmarks, LANDMARKS)
    ql_wide = ql_heads.astype(jnp.float32)
    kl_wide = kl_heads.astype(jnp.float32)
    v_wide = v_heads.astype(jnp.float32)
    first_scores = (
        jnp.einsum("sthd,smhd->shtm", q_heads, kl_heads, preferred_element_type=jnp.float32)
        * scores_factor
    )
    first_kernel = jax.nn.softmax(first_scores, axis=-1)
    kern_low = first_kernel.astype(jnp.bfloat16)
    score_two = (
        jnp.einsum("smhd,snhd->shmn", ql_heads, kl_heads, preferred_element_type=jnp.float32)
        * scores_factor
    )
    second_kernel = jax.nn.softmax(score_two, axis=-1)
    inverse, inverse_back = jax.vjp(newton_schulz_inverse, second_kernel)
    third_scores = (
        jnp.einsum("smhd,sthd->shmt", ql_heads, k_heads, preferred_element_type=jnp.float32)
        * scores_factor
    )
    top_local = jnp.max(third_scores, axis=-1)
    weight_local = jnp.exp(third_scores - top_local[..., None])
    total_local = jnp.sum(weight_local, axis=-1)
    pooled_local = jnp.einsum("shmt,sthd->shmd", weight_local, v_wide, precision=HIGH_ACCURACY)
    top_all, total_all, pooled_all = swap_merge(
        (top_local, total_local, pooled_local), merge_softmax
    )
    segment_means = pooled_all / total_all[..., None]
    log_total = top_all + jnp.log(total_all)
    reduced_mixer = jnp.einsum(
        "shmn,shnd->shmd", inverse, segment_means, precision=HIGH_ACCURACY
    ).astype(jnp.bfloat16)
    landmark_output = jnp.einsum(
        "shtm,shmd->sthd", kern_low, reduced_mixer, preferred_element_type=jnp.float32
    )
    value_rim = padded(value_tokens, (("seq", 1),), half_taps)
    tap_wide = taps_all.astype(jnp.float32)
    band_rows = min(64, tokens)
    band_columns = band_rows + 2 * half_taps
    bands = tokens // band_rows
    offsets = jnp.arange(band_columns)[None, :] - jnp.arange(band_rows)[:, None]
    tap_places = (offsets[None] == jnp.arange(CONV_TAPS)[:, None, None]).astype(jnp.bfloat16)
    back_places = (2 * half_taps - offsets[None] == jnp.arange(CONV_TAPS)[:, None, None]).astype(
        jnp.bfloat16
    )
    toeplitz = jnp.einsum("hj,jpq->hpq", taps_all, tap_places)
    toeplitz_back = jnp.einsum("hj,jpq->hpq", taps_all, back_places)

    def windows(rim):
        return jnp.stack(
            [
                lax.slice_in_dim(rim, i * band_rows, i * band_rows + band_columns, axis=1)
                for i in range(bands)
            ],
            axis=1,
        ).reshape(seqs, bands, band_columns, heads, HEAD_DIM)

    value_windows = windows(value_rim)
    conv_out = jnp.einsum(
        "hpq,sbqhd->sbphd", toeplitz, value_windows, preferred_element_type=jnp.float32
    ).reshape(seqs, tokens, heads, HEAD_DIM)
    attended = (landmark_output + conv_out).reshape(seqs, tokens, model_width).astype(jnp.bfloat16)
    out_part = jnp.dot(attended, out_full, preferred_element_type=jnp.float32)
    gain_one = norm_attn[0].astype(jnp.float32)
    shift_one = norm_attn[1].astype(jnp.float32)
    gain_two = norm_ffn[0].astype(jnp.float32)
    shift_two = norm_ffn[1].astype(jnp.float32)
    resid_one = x_rows.astype(jnp.float32) + out_part + out_bias.astype(jnp.float32)
    normed_one, centered_one, inv_one = norm_apply(resid_one, gain_one, shift_one)
    normed_low = normed_one.astype(jnp.bfloat16)
    hidden_pre = jnp.einsum(
        "ste,gef->stgf", normed_low, hidden_full, preferred_element_type=jnp.float32
    ).reshape(seqs, tokens, shards * hidden_shard) + hid_all.astype(jnp.float32)
    active, gelu_back = jax.vjp(exact_gelu, hidden_pre)
    active_low = active.astype(jnp.bfloat16)
    down_part = jnp.dot(active_low, down_full, preferred_element_type=jnp.float32)
    resid_two = normed_one + down_part + down_bias.astype(jnp.float32)
    normed_two, centered_two, inv_two = norm_apply(resid_two, gain_two, shift_two)
    layer_out = to_positions(normed_two.astype(jnp.bfloat16))
    grad_y = grad_rows.astype(jnp.float32)
    grad_two = norm_back(grad_y, centered_two, inv_two, gain_two)
    norm_ffn_grad = norm_grads(grad_y, centered_two)
    down_low = grad_two.astype(jnp.bfloat16)
    down_bias_grad = jnp.sum(down_low, axis=(0, 1), dtype=jnp.float32)

    def by_shard(source):
        return source.reshape(seqs, tokens, shards, -1)

    w_down_grad = scatter_grad(
        jnp.einsum(
            "stgf,ste->gef", by_shard(active_low), down_low, preferred_element_type=jnp.float32
        )
    )
    grad_active = jnp.einsum("ste,fe->stf", down_low, down_full, preferred_element_type=jnp.float32)
    grad_pre = gelu_back(grad_active)[0].astype(jnp.bfloat16)
    hid_bias_grad = jnp.sum(grad_pre, axis=(0, 1), dtype=jnp.float32)
    w_hidden_grad = scatter_grad(
        jnp.einsum(
            "stgf,ste->gef", by_shard(grad_pre), normed_low, preferred_element_type=jnp.float32
        )
    )
    back_part = jnp.einsum(
        "stgf,gef->ste", by_shard(grad_pre), hidden_full, preferred_element_type=jnp.float32
    )
    grad_in = grad_two + back_part
    grad_one = norm_back(grad_in, centered_one, inv_one, gain_one)
    norm_attn_grad = norm_grads(grad_in, centered_one)
    out_low = grad_one.astype(jnp.bfloat16)
    out_bias_grad = jnp.sum(out_low, axis=(0, 1), dtype=jnp.float32)
    w_output_grad = scatter_grad(
        jnp.einsum(
            "stgd,ste->ged", by_shard(attended), out_low, preferred_element_type=jnp.float32
        )
    )
    grad_att = jnp.einsum(
        "ste,de->std", out_low, out_full, preferred_element_type=jnp.float32
    ).astype(jnp.bfloat16)
    grad_heads = split_heads(grad_att, tokens)
    mixer_part = jnp.einsum(
        "shtm,sthd->shmd", kern_low, grad_heads, preferred_element_type=jnp.float32
    )
    kern_grad = jnp.einsum(
        "sthd,shmd->shtm", grad_heads, reduced_mixer, preferred_element_type=jnp.float32
    )
    score_grad = first_kernel * (
        kern_grad - jnp.sum(first_kernel * kern_grad, axis=-1, keepdims=True)
    )
    score_low = score_grad.astype(jnp.bfloat16)
    query_grad = (
        jnp.einsum("shtm,smhd->sthd", score_low, kl_heads, preferred_element_type=jnp.float32)
        * scores_factor
    )
    kl_part = (
        jnp.einsum("shtm,sthd->smhd", score_low, q_heads, preferred_element_type=jnp.float32)
        * scores_factor
    )
    mixer_grad, kl_grad_one = swap_sum((mixer_part, kl_part))
    inverse_grad = jnp.einsum("shmd,shnd->shmn", mixer_grad, segment_means, precision=HIGH_ACCURACY)
    pooled_grad = jnp.einsum("shmn,shmd->shnd", inverse, mixer_grad, precision=HIGH_ACCURACY)
    kern_two_grad = inverse_back(inverse_grad)[0]
    score_two_grad = second_kernel * (
        kern_two_grad - jnp.sum(second_kernel * kern_two_grad, axis=-1, keepdims=True)
    )
    ql_grad_two = (
        jnp.einsum("shmn,snhd->smhd", score_two_grad, kl_wide, precision=HIGH_ACCURACY)
        * scores_factor
    )
    kl_grad_two = (
        jnp.einsum("shmn,smhd->snhd", score_two_grad, ql_wide, precision=HIGH_ACCURACY)
        * scores_factor
    )
    third_kernel = jnp.exp(third_scores - log_total[..., None])
    kern_three_grad = jnp.einsum("shmd,sthd->shmt", pooled_grad, v_wide, precision=HIGH_ACCURACY)
    row_dot = jnp.sum(pooled_grad * segment_means, axis=-1, keepdims=True)
    score_three_low = (third_kernel * (kern_three_grad - row_dot)).astype(jnp.bfloat16)
    ql_part = (
        jnp.einsum("shmt,sthd->smhd", score_three_low, k_heads, preferred_element_type=jnp.float32)
        * scores_factor
    )
    key_grad = (
        jnp.einsum("shmt,smhd->sthd", score_three_low, ql_heads, preferred_element_type=jnp.float32)
        * scores_factor
    )
    value_grad = jnp.einsum("shmt,shmd->sthd", third_kernel, pooled_grad, precision=HIGH_ACCURACY)
    ql_grad = swap_sum(ql_part) + ql_grad_two
    kl_grad = kl_grad_one + kl_grad_two
    per_count = 1.0 / segment_count[:, :, None]
    ql_spread = ql_grad.reshape(seqs, LANDMARKS, model_width) * per_count
    kl_spread = kl_grad.reshape(seqs, LANDMARKS, model_width) * per_count
    query_grad = query_grad + split_heads(
        jnp.einsum("stm,smd->std", member_wide, ql_spread, precision=HIGH_ACCURACY), tokens
    )
    key_grad = key_grad + split_heads(
        jnp.einsum("stm,smd->std", member_wide, kl_spread, precision=HIGH_ACCURACY), tokens
    )
    grad_windows = windows(padded(grad_att, (("seq", 1),), half_taps))
    value_grad = value_grad + jnp.einsum(
        "hpq,sbqhd->sbphd", toeplitz_back, grad_windows, preferred_element_type=jnp.float32
    ).reshape(seqs, tokens, heads, HEAD_DIM)
    band_sums = jnp.einsum(
        "sbphd,sbqhd->hpq",
        grad_att.reshape(seqs, bands, band_rows, heads, HEAD_DIM),
        value_windows,
        preferred_element_type=jnp.float32,
    )
    skewed = jnp.pad(band_sums.reshape(heads, band_rows * band_columns), ((0, 0), (0, band_rows)))
    taps_grad = jnp.sum(skewed.reshape(heads, band_rows, band_columns + 1), axis=1)[:, :CONV_TAPS]
    grads_qkv = jnp.stack([query_grad, key_grad, value_grad], axis=3).astype(jnp.bfloat16)
    proj_bias_grad = jnp.sum(grads_qkv[:, :, :, 0::2], axis=(0, 1), dtype=jnp.float32)
    proj_bias_grad = jnp.swapaxes(proj_bias_grad, 0, 1).reshape(2, model_width)
    w_project_grad = scatter_grad(
        jnp.einsum(
            "stgr,ste->ger", by_shard(grads_qkv), x_rows, preferred_element_type=jnp.float32
        )
    )
    input_part = jnp.einsum(
        "sthcf,hcfe->ste", grads_qkv, proj_full, preferred_element_type=jnp.float32
    )
    input_grad = to_positions((input_part + grad_one).astype(jnp.bfloat16))
    small_list = [
        proj_bias_grad,
        taps_grad,
        out_bias_grad,
        norm_attn_grad,
        hid_bias_grad,
        down_bias_grad,
        norm_ffn_grad,
    ]
    small_sum = lax.psum(
        jnp.concatenate([part.reshape(-1) for part in small_list]), ("row", "seq", "head")
    )
    outs, start_at = [], 0
    for part in small_list:
        outs.append(small_sum[start_at : start_at + part.size].reshape(part.shape))
        start_at += part.size

    def own_share(source, axis):
        size = source.shape[axis] // shards
        return lax.dynamic_slice_in_dim(source, head_place * size, size, axis=axis)

    return (
        layer_out,
        input_grad,
        w_project_grad.T.reshape(heads_shard, 3, HEAD_DIM, -1),
        own_share(outs[0], 1),
        own_share(outs[1], 0),
        w_output_grad.T,
        own_share(outs[2], 0),
        own_share(outs[3], 1),
        w_hidden_grad,
        own_share(outs[4], 0),
        w_down_grad.T,
        own_share(outs[5], 0),
        own_share(outs[6], 1),
    )


def solution(mesh):
    in_specs = (
        P("row", ("seq", "head"), None),
        P("row", "seq"),
        P("head", None, None, None),
        P(None, "head"),
        P("head", None),
        P("head", None),
        P(),
        P(),
        P(None, "head"),
        P("head"),
        P("head", None),
        P(),
        P(),
        P("row", ("seq", "head"), None),
    )
    out_specs = (
        P("row", ("seq", "head"), None),
        P("row", ("seq", "head"), None),
        P("head", None, None, ("row", "seq")),
        P(None, "head"),
        P("head", None),
        P("head", ("row", "seq")),
        P("head"),
        P(None, "head"),
        P(("row", "seq"), "head"),
        P("head"),
        P("head", ("row", "seq")),
        P("head"),
        P(None, "head"),
    )
    return jax.shard_map(
        on_device, mesh=mesh, in_specs=in_specs, out_specs=out_specs, check_vma=False
    )
```

```python
import jax
import jax.numpy as jnp
from jax import lax
from jax.experimental import pallas as pl
from jax.experimental.pallas import tpu as pltpu
from jax.sharding import PartitionSpec as P

HEAD_DIM = 64
LANDMARKS = 64
CONV_TAPS = 33
NEWTON_STEPS = 6


EPS = 1e-05
HIGH_ACCURACY = lax.Precision.HIGHEST


def combined_all(part, axis, combine):
    gathered = jax.tree.map(lambda a: lax.all_gather(a, axis), part)

    def take(source):
        return jax.tree.map(lambda a: lax.dynamic_index_in_dim(a, source, 0, False), gathered)

    return lax.fori_loop(
        1, lax.axis_size(axis), lambda source, state: combine(state, take(source)), take(0)
    )


def padded(cells, sides, width):
    for axis, dim in sides:
        count = lax.axis_size(axis)
        ends = count - 1
        head = lax.slice_in_dim(cells, 0, width, axis=dim)
        tail = lax.slice_in_dim(cells, cells.shape[dim] - width, cells.shape[dim], axis=dim)
        cells = jnp.concatenate(
            [
                lax.ppermute(tail, axis, [(i, (i + 1) % count) for i in range(ends)]),
                cells,
                lax.ppermute(head, axis, [((i + 1) % count, i) for i in range(ends)]),
            ],
            axis=dim,
        )
    return cells


def newton_schulz_inverse(kernel):
    order_size = LANDMARKS
    identity = jnp.eye(kernel.shape[-1], dtype=jnp.float32)
    estimate = jnp.swapaxes(kernel, -1, -2) / order_size
    for repeat in range(NEWTON_STEPS):
        product = jnp.einsum("...ij,...jk->...ik", kernel, estimate, precision=HIGH_ACCURACY)
        nested = 7.0 * identity - product
        nested = 15.0 * identity - jnp.einsum(
            "...ij,...jk->...ik", product, nested, precision=HIGH_ACCURACY
        )
        nested = 13.0 * identity - jnp.einsum(
            "...ij,...jk->...ik", product, nested, precision=HIGH_ACCURACY
        )
        estimate = 0.25 * jnp.einsum(
            "...ij,...jk->...ik", estimate, nested, precision=HIGH_ACCURACY
        )
    return estimate


def exact_gelu(pre_act):
    return jax.nn.gelu(pre_act, approximate=False)


def merge_softmax(former, latter):
    top_one, total_one, pooled_one = former
    top_two, total_two, pooled_two = latter
    top_new = jnp.maximum(top_one, top_two)
    factor_one = jnp.exp(top_one - top_new)
    factor_two = jnp.exp(top_two - top_new)
    return (
        top_new,
        total_one * factor_one + total_two * factor_two,
        pooled_one * factor_one[..., None] + pooled_two * factor_two[..., None],
    )


PAIR = 2 * HEAD_DIM
SCALE = HEAD_DIM ** (-0.5)
HALF_TAPS = CONV_TAPS // 2


def dot_on(a, b, dim_a, dim_b):
    return lax.dot_general(
        a, b, (((dim_a,), (dim_b,)), ((), ())), preferred_element_type=jnp.float32
    )


def split_low(wide):
    high = wide.astype(jnp.bfloat16)
    return high, (wide - high.astype(jnp.float32)).astype(jnp.bfloat16)


def second_half(shape, dim):
    return lax.broadcasted_iota(jnp.int32, shape, dim) >= HEAD_DIM


def same_head(shape=(PAIR, PAIR)):
    return second_half(shape, 0) == second_half(shape, 1)


def pair_rows(block):
    wide = block.astype(jnp.float32)
    both = jnp.concatenate([wide, wide], axis=0)
    return jnp.where(same_head(), both, 0.0).astype(block.dtype)


def by_half(values, combine, neutral):
    late = second_half(values.shape, 1)
    first = combine(jnp.where(late, neutral, values), axis=1, keepdims=True)
    last = combine(jnp.where(late, values, neutral), axis=1, keepdims=True)
    return jnp.where(late, last, first)


def first_softmax(query, key_marks):
    scores = dot_on(query, key_marks, 1, 1) * SCALE
    powers = jnp.exp(scores - by_half(scores, jnp.max, -jnp.inf))
    return powers / by_half(powers, jnp.sum, 0.0)


def banded(toeplitz_ref, rim_ref, tokens):
    rows = toeplitz_ref.shape[1]
    columns = toeplitz_ref.shape[2]
    bands = []
    for start in range(0, tokens, rows):
        window = rim_ref[start : start + columns, :]
        first = dot_on(toeplitz_ref[0], window, 1, 0)
        last = dot_on(toeplitz_ref[1], window, 1, 0)
        bands.append(jnp.where(second_half(first.shape, 1), last, first))
    return jnp.concatenate(bands, axis=0) if len(bands) > 1 else bands[0]


def pool_kernel(key_ref, value_ref, ql_ref, pooled_ref, stats_ref):
    scores = dot_on(pair_rows(ql_ref[...]), key_ref[...], 1, 1) * SCALE
    top = jnp.max(scores, axis=1, keepdims=True)
    powers = jnp.exp(scores - top)
    total = jnp.sum(powers, axis=1, keepdims=True)
    high, low = split_low(powers)
    pooled = dot_on(high, value_ref[...], 1, 0) + dot_on(low, value_ref[...], 1, 0)
    pooled_ref[0] = jnp.where(same_head(), pooled, 0.0)
    late = second_half((PAIR, PAIR), 1)
    stats_ref[0] = jnp.where(late, jnp.broadcast_to(total, late.shape), top)


def attend_kernel(query_ref, rim_ref, kl_ref, mixer_ref, toeplitz_ref, attended_ref):
    kernel = first_softmax(query_ref[...], pair_rows(kl_ref[...])).astype(jnp.bfloat16)
    mixed = dot_on(kernel, mixer_ref[0], 1, 0)
    tokens = query_ref.shape[0]
    attended_ref[...] = (mixed + banded(toeplitz_ref, rim_ref, tokens)).astype(jnp.bfloat16)


def query_back_kernel(
    query_ref, grad_ref, kl_ref, mixer_ref, mixer_part_ref, kl_part_ref, query_grad_ref
):
    key_marks = pair_rows(kl_ref[...])
    kernel = first_softmax(query_ref[...], key_marks)
    mixer_part = dot_on(kernel.astype(jnp.bfloat16), grad_ref[...], 0, 0)
    mixer_part_ref[0] = jnp.where(same_head(), mixer_part, 0.0)
    kern_grad = dot_on(grad_ref[...], mixer_ref[0], 1, 1)
    score_grad = kernel * (kern_grad - by_half(kernel * kern_grad, jnp.sum, 0.0))
    score_low = score_grad.astype(jnp.bfloat16)
    query_grad_ref[...] = dot_on(score_low, key_marks, 1, 0) * SCALE
    kl_part = dot_on(score_low, query_ref[...], 0, 0) * SCALE
    kl_part_ref[0] = jnp.where(same_head(), kl_part, 0.0)


def key_back_kernel(
    key_ref,
    value_ref,
    value_rim_ref,
    grad_ref,
    grad_rim_ref,
    ql_ref,
    pooled_grad_ref,
    means_ref,
    log_ref,
    toeplitz_ref,
    ql_part_ref,
    key_grad_ref,
    value_grad_ref,
    band_ref,
):
    query_marks = pair_rows(ql_ref[...])
    scores = dot_on(query_marks, key_ref[...], 1, 1) * SCALE
    kernel = jnp.exp(scores - log_ref[0][:, :1])
    grad_high, grad_low = split_low(pooled_grad_ref[0])
    kern_grad = dot_on(grad_high, value_ref[...], 1, 1) + dot_on(grad_low, value_ref[...], 1, 1)
    row_dot = jnp.sum(pooled_grad_ref[0] * means_ref[0], axis=1, keepdims=True)
    score_low = (kernel * (kern_grad - row_dot)).astype(jnp.bfloat16)
    ql_part = dot_on(score_low, key_ref[...], 1, 0) * SCALE
    ql_part_ref[0] = jnp.where(same_head(), ql_part, 0.0)
    key_grad_ref[...] = dot_on(score_low, query_marks, 0, 0) * SCALE
    kern_high, kern_low = split_low(kernel)
    value_grad = (
        dot_on(kern_high, grad_high, 0, 0)
        + dot_on(kern_high, grad_low, 0, 0)
        + dot_on(kern_low, grad_high, 0, 0)
    )
    tokens = key_ref.shape[0]
    rows, columns = toeplitz_ref.shape[1:]
    value_grad_ref[...] = (value_grad + banded(toeplitz_ref, grad_rim_ref, tokens)).astype(
        jnp.bfloat16
    )
    first = jnp.zeros((rows, columns), jnp.float32)
    last = first
    for start in range(0, tokens, rows):
        grads = grad_ref[start : start + rows, :]
        late = second_half(grads.shape, 1)
        window = value_rim_ref[start : start + columns, :]
        wide = grads.astype(jnp.float32)
        first = first + dot_on(jnp.where(late, 0.0, wide).astype(jnp.bfloat16), window, 1, 1)
        last = last + dot_on(jnp.where(late, wide, 0.0).astype(jnp.bfloat16), window, 1, 1)
    band_ref[0] = first
    band_ref[1] = last


def pair_call(body, operands, results):
    pairs = operands[0][0].shape[1] // PAIR

    def spec(kind, shape):
        if kind == "lanes":
            return pl.BlockSpec((shape[0], PAIR), lambda i: (0, i))
        if kind == "pair":
            return pl.BlockSpec((1,) + shape[1:], lambda i: (i, 0, 0))
        return pl.BlockSpec((2,) + shape[1:], lambda i: (i, 0, 0))

    flops = 2 * 12 * pairs * operands[0][0].shape[0] * PAIR * PAIR
    moved = 8 * sum(array.size for array, _ in operands)
    return pl.pallas_call(
        body,
        grid=(pairs,),
        in_specs=[spec(kind, array.shape) for array, kind in operands],
        out_specs=[spec(kind, shape) for shape, _, kind in results],
        out_shape=[jax.ShapeDtypeStruct(shape, dtype) for shape, dtype, _ in results],
        cost_estimate=pl.CostEstimate(flops=flops, bytes_accessed=moved, transcendentals=0),
    )(*[array for array, _ in operands])


def swap_sum(tree):
    if lax.axis_size("seq") == 2:
        other = jax.tree.map(lambda a: lax.ppermute(a, "seq", [(0, 1), (1, 0)]), tree)
        return jax.tree.map(lambda a, b: a + b, tree, other)
    return lax.psum(tree, "seq")


def swap_merge(part, combine):
    if lax.axis_size("seq") == 2:
        other = jax.tree.map(lambda a: lax.ppermute(a, "seq", [(0, 1), (1, 0)]), part)
        return combine(part, other)
    return combined_all(part, "seq", combine)


def to_documents(rows):
    blocks = lax.all_to_all(rows, "head", split_axis=0, concat_axis=0, tiled=True)
    return blocks.reshape(1, -1, rows.shape[2])


def to_positions(rows):
    blocks = rows.reshape(lax.axis_size("head"), -1, rows.shape[2])
    return lax.all_to_all(blocks, "head", split_axis=0, concat_axis=0, tiled=True)


def shifted(tree, axis, step):
    count = lax.axis_size(axis)
    links = [(i, (i + step) % count) for i in range(count)]
    return jax.tree.map(lambda a: lax.ppermute(a, axis, links), tree)


def block_before(axis, step):
    return lax.rem(lax.axis_index(axis) + lax.axis_size(axis) - step, lax.axis_size(axis))


def block_after(axis, step):
    return lax.rem(lax.axis_index(axis) + step, lax.axis_size(axis))


def gather_small(packed):
    return jnp.stack(
        [packed] + [shifted(packed, "head", k) for k in range(1, lax.axis_size("head"))]
    )


def gather_over_head(shard):
    rows, columns = shard.shape
    shares = lax.axis_size("row") * lax.axis_size("seq")
    place = lax.axis_index("row") * lax.axis_size("seq") + lax.axis_index("seq")
    piece = lax.dynamic_index_in_dim(
        shard.reshape(shares, rows // shares, columns), place, 0, False
    )
    return jnp.stack([shifted(piece, "head", k) for k in range(1, lax.axis_size("head"))])


def gather_over_row(others):
    return [others] + [shifted(others, "row", k) for k in range(1, lax.axis_size("row"))]


def gather_over_seq(shard, shares):
    size_row, size_seq = lax.axis_size("row"), lax.axis_size("seq")
    shards = lax.axis_size("head")
    _, share_rows, columns = shares[0].shape
    full = jnp.zeros((shards, size_row, size_seq, share_rows, columns), shard.dtype)
    full = lax.dynamic_update_slice(
        full, shard.reshape((1,) + full.shape[1:]), (0, 0, 0, 0, 0)
    )
    for k in range(size_row):
        at_row = block_before("row", k)
        for j in range(size_seq):
            block = shares[k] if j == 0 else shifted(shares[k], "seq", j)
            full = lax.dynamic_update_slice(
                full, block[:, None, None], (1, at_row, block_before("seq", j), 0, 0)
            )
    return full.reshape(-1, columns)


def sum_blocks(blocks, axis, dim):
    total = lax.dynamic_index_in_dim(blocks, lax.axis_index(axis), dim, False).astype(jnp.float32)
    for k in range(1, lax.axis_size(axis)):
        sent = lax.dynamic_index_in_dim(blocks, block_after(axis, k), dim, False)
        total = total + shifted(sent, axis, k).astype(jnp.float32)
    return total


def sum_shards(blocks):
    count = lax.axis_size("head")
    total = blocks[0].astype(jnp.float32)
    for k in range(1, count):
        total = total + shifted(blocks[k], "head", count - k).astype(jnp.float32)
    return total


def grad_over_seq(grad):
    features, columns = grad.shape
    size_row, size_seq = lax.axis_size("row"), lax.axis_size("seq")
    low = grad.reshape(size_row, size_seq, features // (size_row * size_seq), columns)
    return sum_blocks(low, "seq", 1).astype(jnp.bfloat16)


def grad_over_rest(low):
    low = sum_blocks(low, "row", 0).astype(jnp.bfloat16)
    return sum_shards(jnp.split(low, lax.axis_size("head"), axis=1))


def sum_everywhere(values, axis):
    total = values
    for k in range(1, lax.axis_size(axis)):
        total = total + shifted(values, axis, k)
    return total


def norm_apply(residual, gain_row, shift_row):
    former = jnp.mean(residual, axis=-1)
    centered_raw = residual - former[..., None]
    variance = jnp.mean(centered_raw * centered_raw, axis=-1)
    inv_dev = lax.rsqrt(variance + EPS)
    centered = centered_raw * inv_dev[..., None]
    return (centered * gain_row + shift_row, centered, inv_dev)


def norm_back(incoming, centered, inv_dev, gain_row):
    scaled = incoming * gain_row
    former = jnp.mean(scaled, axis=-1)
    latter = jnp.mean(scaled * centered, axis=-1)
    return inv_dev[..., None] * (scaled - former[..., None] - centered * latter[..., None])


def norm_grads(incoming, centered):
    return jnp.stack([jnp.sum(incoming * centered, axis=(0, 1)), jnp.sum(incoming, axis=(0, 1))])


def on_device(
    inputs,
    segment_ids,
    w_project,
    proj_bias,
    conv_taps,
    w_output,
    out_bias,
    norm_attn,
    w_hidden,
    hid_bias,
    w_down,
    down_bias,
    norm_ffn,
    cotangent,
):
    model_width = inputs.shape[2]
    shards = lax.axis_size("head")
    heads_shard = w_project.shape[0]
    heads = heads_shard * shards
    hidden_shard = w_hidden.shape[1]
    width_shard = heads_shard * HEAD_DIM
    head_place = lax.axis_index("head")

    x_rows = to_documents(inputs)
    seqs, tokens, _ = x_rows.shape
    small_pack = jnp.concatenate([proj_bias.reshape(-1), conv_taps.reshape(-1), hid_bias])
    small_all = gather_small(small_pack)
    split_one = 2 * width_shard
    split_two = split_one + heads_shard * CONV_TAPS
    bias_all = small_all[:, :split_one].reshape(shards, 2, width_shard)
    bias_all = jnp.swapaxes(bias_all, 0, 1).reshape(2, model_width)
    taps_all = small_all[:, split_one:split_two].reshape(heads, CONV_TAPS)
    hid_all = small_all[:, split_two:].reshape(shards * hidden_shard)

    proj_rows = jnp.swapaxes(w_project, 0, 1).reshape(3 * width_shard, model_width)
    pin = lax.optimization_barrier
    first_shard = jnp.concatenate([proj_rows, w_output], axis=0)
    first_shares = gather_over_head(first_shard)
    hidden_shard_t, first_shares = pin((w_hidden.T, first_shares))
    hidden_shares = gather_over_head(hidden_shard_t)
    first_shares = gather_over_row(first_shares)
    down_shard, hidden_shares, first_shares = pin((w_down, hidden_shares, first_shares))
    down_shares = gather_over_head(down_shard)
    hidden_shares = gather_over_row(hidden_shares)
    proj_out = gather_over_seq(first_shard, first_shares).reshape(shards, -1, model_width)
    proj_full = proj_out[:, : 3 * width_shard].reshape(shards, 3, width_shard, model_width)
    out_full = proj_out[:, 3 * width_shard :].reshape(model_width, model_width)
    grad_rows = to_documents(cotangent)

    segment_rows = lax.dynamic_slice_in_dim(segment_ids, head_place * seqs, seqs, axis=0)

    mixed_proj = [
        jnp.einsum(
            "ste,gfe->stgf", x_rows, proj_full[:, c], preferred_element_type=jnp.float32
        ).reshape(seqs, tokens, model_width)
        for c in range(3)
    ]
    query_tokens = (mixed_proj[0] + bias_all[0]).astype(jnp.bfloat16)
    key_tokens = mixed_proj[1].astype(jnp.bfloat16)
    value_tokens = (mixed_proj[2] + bias_all[1]).astype(jnp.bfloat16)
    query_tokens, hidden_shares, down_shares = pin((query_tokens, hidden_shares, down_shares))
    down_shares = gather_over_row(down_shares)
    hidden_full = gather_over_seq(hidden_shard_t, hidden_shares)
    segment_membership = (
        segment_rows[:, :, None] == jnp.arange(LANDMARKS, dtype=jnp.int32)[None, None, :]
    )
    member_low = segment_membership.astype(jnp.bfloat16)
    member_wide = segment_membership.astype(jnp.float32)
    query_sums = jnp.einsum(
        "stm,std->smd", member_low, query_tokens, preferred_element_type=jnp.float32
    )
    key_sums = jnp.einsum(
        "stm,std->smd", member_low, key_tokens, preferred_element_type=jnp.float32
    )
    segment_count = jnp.sum(member_wide, axis=1)
    query_sums, key_sums, segment_count = swap_sum((query_sums, key_sums, segment_count))
    query_landmarks = (query_sums / segment_count[:, :, None]).astype(jnp.bfloat16)
    key_landmarks = (key_sums / segment_count[:, :, None]).astype(jnp.bfloat16)
    pairs = model_width // PAIR
    q_all, k_all, v_all = query_tokens[0], key_tokens[0], value_tokens[0]
    ql_all, kl_all = query_landmarks[0], key_landmarks[0]
    own_head = same_head()

    def paired(marks):
        blocks = jnp.swapaxes(marks.reshape(LANDMARKS, pairs, PAIR), 0, 1)
        both = jnp.concatenate([blocks, blocks], axis=1)
        return jnp.where(own_head, both, jnp.zeros_like(both))

    def unpaired(blocks):
        marks = blocks[:, :LANDMARKS] + blocks[:, LANDMARKS:]
        return jnp.swapaxes(marks, 0, 1).reshape(LANDMARKS, model_width)

    ql_pairs, kl_pairs = paired(ql_all), paired(kl_all)
    score_two = jnp.einsum("gmd,gnd->gmn", ql_pairs, kl_pairs, preferred_element_type=jnp.float32)
    score_two = jnp.where(own_head, score_two * SCALE, -jnp.inf)
    second_kernel = jax.nn.softmax(score_two, axis=-1)
    inverse, inverse_back = jax.vjp(newton_schulz_inverse, second_kernel)
    square = (pairs, PAIR, PAIR)
    pooled_local, stats_local = pair_call(
        pool_kernel,
        [(k_all, "lanes"), (v_all, "lanes"), (ql_all, "lanes")],
        [(square, jnp.float32, "pair"), (square, jnp.float32, "pair")],
    )
    pooled_local, down_shares = pin((pooled_local, down_shares))
    down_full = gather_over_seq(down_shard, down_shares)
    top_all, total_all, pooled_all = swap_merge(
        (stats_local[:, :, 0], stats_local[:, :, HEAD_DIM], pooled_local), merge_softmax
    )
    segment_means = pooled_all / total_all[..., None]
    log_total = jnp.broadcast_to((top_all + jnp.log(total_all))[..., None], square)
    reduced_mixer = jnp.einsum(
        "gmn,gnd->gmd", inverse, segment_means, precision=HIGH_ACCURACY
    ).astype(jnp.bfloat16)
    value_rim = padded(value_tokens, (("seq", 1),), HALF_TAPS)[0]
    band_rows = min(128, tokens)
    band_columns = band_rows + 2 * HALF_TAPS
    offsets = jnp.arange(band_columns)[None, :] - jnp.arange(band_rows)[:, None]
    tap_places = (offsets[None] == jnp.arange(CONV_TAPS)[:, None, None]).astype(jnp.bfloat16)
    toeplitz = jnp.einsum("hj,jpq->hpq", taps_all, tap_places)
    toeplitz_back = jnp.einsum("hj,jpq->hpq", taps_all[:, ::-1], tap_places)
    attended = pair_call(
        attend_kernel,
        [
            (q_all, "lanes"),
            (value_rim, "lanes"),
            (kl_all, "lanes"),
            (reduced_mixer, "pair"),
            (toeplitz, "heads"),
        ],
        [((tokens, model_width), jnp.bfloat16, "lanes")],
    )[0][None]
    out_part = jnp.dot(attended, out_full, preferred_element_type=jnp.float32)
    gain_one = norm_attn[0].astype(jnp.float32)
    shift_one = norm_attn[1].astype(jnp.float32)
    gain_two = norm_ffn[0].astype(jnp.float32)
    shift_two = norm_ffn[1].astype(jnp.float32)
    resid_one = x_rows.astype(jnp.float32) + out_part + out_bias.astype(jnp.float32)
    normed_one, centered_one, inv_one = norm_apply(resid_one, gain_one, shift_one)
    normed_low = normed_one.astype(jnp.bfloat16)
    hidden_pre = jnp.einsum(
        "ste,fe->stf", normed_low, hidden_full, preferred_element_type=jnp.float32
    ) + hid_all.astype(jnp.float32)
    active, gelu_back = jax.vjp(exact_gelu, hidden_pre)
    active_low = active.astype(jnp.bfloat16)
    down_part = jnp.dot(active_low, down_full, preferred_element_type=jnp.float32)
    resid_two = normed_one + down_part + down_bias.astype(jnp.float32)
    normed_two, centered_two, inv_two = norm_apply(resid_two, gain_two, shift_two)
    layer_out = to_positions(normed_two.astype(jnp.bfloat16))
    grad_y = grad_rows.astype(jnp.float32)
    grad_two = norm_back(grad_y, centered_two, inv_two, gain_two)
    norm_ffn_grad = norm_grads(grad_y, centered_two)
    down_low = grad_two.astype(jnp.bfloat16)
    down_bias_grad = jnp.sum(down_low, axis=(0, 1), dtype=jnp.float32)

    down_low, down_start = lax.optimization_barrier(
        (
            down_low,
            jnp.einsum(
                "stf,ste->ef", active_low, down_low, preferred_element_type=jnp.float32
            ).astype(jnp.bfloat16),
        )
    )
    down_start = grad_over_seq(down_start)
    grad_active = jnp.einsum("ste,fe->stf", down_low, down_full, preferred_element_type=jnp.float32)
    grad_pre = gelu_back(grad_active)[0].astype(jnp.bfloat16)
    hid_bias_grad = jnp.sum(grad_pre, axis=(0, 1), dtype=jnp.float32)
    grad_pre, hidden_start = lax.optimization_barrier(
        (
            grad_pre,
            jnp.einsum(
                "stf,ste->ef", grad_pre, normed_low, preferred_element_type=jnp.float32
            ).astype(jnp.bfloat16),
        )
    )
    hidden_start = grad_over_seq(hidden_start)
    back_part = jnp.einsum(
        "stf,fe->ste", grad_pre, hidden_full, preferred_element_type=jnp.float32
    )
    grad_in = grad_two + back_part
    grad_one = norm_back(grad_in, centered_one, inv_one, gain_one)
    norm_attn_grad = norm_grads(grad_in, centered_one)
    out_low = grad_one.astype(jnp.bfloat16)
    out_bias_grad = jnp.sum(out_low, axis=(0, 1), dtype=jnp.float32)
    out_low, down_start, out_start = lax.optimization_barrier(
        (
            out_low,
            down_start,
            jnp.einsum(
                "std,ste->ed", attended, out_low, preferred_element_type=jnp.float32
            ).astype(jnp.bfloat16),
        )
    )
    out_start = grad_over_seq(out_start)
    grad_att = jnp.einsum(
        "ste,de->std", out_low, out_full, preferred_element_type=jnp.float32
    ).astype(jnp.bfloat16)
    grad_att, hidden_start = lax.optimization_barrier((grad_att, hidden_start))
    w_down_grad = grad_over_rest(down_start)
    w_hidden_grad = grad_over_rest(hidden_start)
    w_output_grad = grad_over_rest(out_start)
    mixer_part, kl_part, query_grad = pair_call(
        query_back_kernel,
        [(q_all, "lanes"), (grad_att[0], "lanes"), (kl_all, "lanes"), (reduced_mixer, "pair")],
        [
            (square, jnp.float32, "pair"),
            (square, jnp.float32, "pair"),
            ((tokens, model_width), jnp.float32, "lanes"),
        ],
    )
    grad_rim = padded(grad_att, (("seq", 1),), HALF_TAPS)[0]
    mixer_grad, kl_grad_one = swap_sum((mixer_part, kl_part))
    inverse_grad = jnp.einsum("gmd,gnd->gmn", mixer_grad, segment_means, precision=HIGH_ACCURACY)
    pooled_grad = jnp.einsum("gmn,gmd->gnd", inverse, mixer_grad, precision=HIGH_ACCURACY)
    ql_part, key_grad, value_grad, band_sums = pair_call(
        key_back_kernel,
        [
            (k_all, "lanes"),
            (v_all, "lanes"),
            (value_rim, "lanes"),
            (grad_att[0], "lanes"),
            (grad_rim, "lanes"),
            (ql_all, "lanes"),
            (pooled_grad, "pair"),
            (segment_means, "pair"),
            (log_total, "pair"),
            (toeplitz_back, "heads"),
        ],
        [
            (square, jnp.float32, "pair"),
            ((tokens, model_width), jnp.float32, "lanes"),
            ((tokens, model_width), jnp.bfloat16, "lanes"),
            ((heads, band_rows, band_columns), jnp.float32, "heads"),
        ],
    )
    kern_two_grad = inverse_back(inverse_grad)[0]
    score_two_grad = second_kernel * (
        kern_two_grad - jnp.sum(second_kernel * kern_two_grad, axis=-1, keepdims=True)
    )
    ql_grad_two = jnp.einsum(
        "gmn,gnd->gmd", score_two_grad, kl_pairs.astype(jnp.float32), precision=HIGH_ACCURACY
    )
    kl_grad_two = jnp.einsum(
        "gmn,gmd->gnd", score_two_grad, ql_pairs.astype(jnp.float32), precision=HIGH_ACCURACY
    )
    ql_grad = unpaired(swap_sum(ql_part) + ql_grad_two * SCALE)
    kl_grad = unpaired(kl_grad_one + kl_grad_two * SCALE)
    per_count = 1.0 / segment_count[0][:, None]
    spreads = jnp.concatenate([ql_grad * per_count, kl_grad * per_count], axis=1)
    spread_high, spread_low = split_low(spreads)
    spread_rows = jnp.dot(
        member_low[0], spread_high, preferred_element_type=jnp.float32
    ) + jnp.dot(member_low[0], spread_low, preferred_element_type=jnp.float32)
    query_grad = query_grad + spread_rows[:, :model_width]
    key_grad = key_grad + spread_rows[:, model_width:]
    skewed = jnp.pad(band_sums.reshape(heads, band_rows * band_columns), ((0, 0), (0, band_rows)))
    taps_grad = jnp.sum(skewed.reshape(heads, band_rows, band_columns + 1), axis=1)[:, :CONV_TAPS]
    grads_qkv = jnp.stack(
        [
            part.astype(jnp.bfloat16).reshape(seqs, tokens, shards, width_shard)
            for part in (query_grad, key_grad, value_grad)
        ],
        axis=3,
    )
    proj_bias_grad = jnp.sum(grads_qkv[:, :, :, 0::2], axis=(0, 1), dtype=jnp.float32)
    proj_start = jnp.einsum(
        "str,ste->er", grads_qkv.reshape(seqs, tokens, -1), x_rows, preferred_element_type=jnp.float32
    ).astype(jnp.bfloat16)
    w_project_grad = grad_over_rest(grad_over_seq(proj_start))
    input_part = jnp.einsum(
        "stgcf,gcfe->ste", grads_qkv, proj_full, preferred_element_type=jnp.float32
    )
    input_grad = to_positions((input_part + grad_one).astype(jnp.bfloat16))

    def by_place(source):
        blocks = source.reshape(-1, shards, width_shard)
        return jnp.stack(
            [
                lax.dynamic_index_in_dim(blocks, block_before("head", k), 1, False).reshape(-1)
                for k in range(shards)
            ]
        )

    small_list = [
        proj_bias_grad.reshape(shards, -1),
        taps_grad.reshape(shards, -1),
        by_place(out_bias_grad),
        by_place(norm_attn_grad),
        hid_bias_grad.reshape(shards, -1),
        by_place(down_bias_grad),
        by_place(norm_ffn_grad),
    ]
    small_sum = jnp.concatenate(small_list, axis=1)
    small_sum = sum_shards(sum_everywhere(sum_everywhere(small_sum, "seq"), "row"))
    outs, start_at = [], 0
    for part in small_list:
        outs.append(small_sum[start_at : start_at + part.shape[1]])
        start_at += part.shape[1]

    return (
        layer_out,
        input_grad,
        jnp.swapaxes(w_project_grad.T.reshape(3, heads_shard, HEAD_DIM, -1), 0, 1),
        outs[0].reshape(2, width_shard),
        outs[1].reshape(heads_shard, CONV_TAPS),
        w_output_grad.T,
        outs[2],
        outs[3].reshape(2, width_shard),
        w_hidden_grad,
        outs[4],
        w_down_grad.T,
        outs[5],
        outs[6].reshape(2, width_shard),
    )


def solution(mesh):
    in_specs = (
        P("row", ("seq", "head"), None),
        P("row", "seq"),
        P("head", None, None, None),
        P(None, "head"),
        P("head", None),
        P("head", None),
        P(),
        P(),
        P(None, "head"),
        P("head"),
        P("head", None),
        P(),
        P(),
        P("row", ("seq", "head"), None),
    )
    out_specs = (
        P("row", ("seq", "head"), None),
        P("row", ("seq", "head"), None),
        P("head", None, None, ("row", "seq")),
        P(None, "head"),
        P("head", None),
        P("head", ("row", "seq")),
        P("head"),
        P(None, "head"),
        P(("row", "seq"), "head"),
        P("head"),
        P("head", ("row", "seq")),
        P("head"),
        P(None, "head"),
    )
    return jax.shard_map(
        on_device, mesh=mesh, in_specs=in_specs, out_specs=out_specs, check_vma=False
    )
```

```python
import jax
import jax.numpy as jnp
from jax import lax
from jax.experimental import pallas as pl
from jax.experimental.pallas import tpu as pltpu
from jax.sharding import PartitionSpec as P

HEAD_DIM = 64
LANDMARKS = 64
CONV_TAPS = 33
NEWTON_STEPS = 6


EPS = 1e-05
HIGH_ACCURACY = lax.Precision.HIGHEST


def combined_all(part, axis, combine):
    gathered = jax.tree.map(lambda a: lax.all_gather(a, axis), part)

    def take(source):
        return jax.tree.map(lambda a: lax.dynamic_index_in_dim(a, source, 0, False), gathered)

    return lax.fori_loop(
        1, lax.axis_size(axis), lambda source, state: combine(state, take(source)), take(0)
    )


def padded(cells, sides, width):
    for axis, dim in sides:
        count = lax.axis_size(axis)
        ends = count - 1
        head = lax.slice_in_dim(cells, 0, width, axis=dim)
        tail = lax.slice_in_dim(cells, cells.shape[dim] - width, cells.shape[dim], axis=dim)
        cells = jnp.concatenate(
            [
                lax.ppermute(tail, axis, [(i, (i + 1) % count) for i in range(ends)]),
                cells,
                lax.ppermute(head, axis, [((i + 1) % count, i) for i in range(ends)]),
            ],
            axis=dim,
        )
    return cells


def with_rims(cells, width):
    if lax.axis_size("seq") != 2:
        return padded(cells, (("seq", 1),), width)
    first = lax.axis_index("seq") == 0
    sent = jnp.where(first, cells[:, -width:], cells[:, :width])
    got = lax.ppermute(sent, "seq", [(0, 1), (1, 0)])
    none = jnp.zeros_like(got)
    return jnp.concatenate(
        [jnp.where(first, none, got), cells, jnp.where(first, got, none)], axis=1
    )


def newton_schulz_inverse(kernel):
    order_size = LANDMARKS
    identity = jnp.eye(kernel.shape[-1], dtype=jnp.float32)
    estimate = jnp.swapaxes(kernel, -1, -2) / order_size
    for repeat in range(NEWTON_STEPS):
        product = jnp.einsum("...ij,...jk->...ik", kernel, estimate, precision=lax.Precision.HIGH)
        nested = 7.0 * identity - product
        nested = 15.0 * identity - jnp.einsum(
            "...ij,...jk->...ik", product, nested, precision=lax.Precision.HIGH
        )
        nested = 13.0 * identity - jnp.einsum(
            "...ij,...jk->...ik", product, nested, precision=lax.Precision.HIGH
        )
        estimate = 0.25 * jnp.einsum(
            "...ij,...jk->...ik", estimate, nested, precision=lax.Precision.HIGH
        )
    return estimate


def exact_gelu(pre_act):
    return jax.nn.gelu(pre_act, approximate=False)


def merge_softmax(former, latter):
    top_one, total_one, pooled_one = former
    top_two, total_two, pooled_two = latter
    top_new = jnp.maximum(top_one, top_two)
    factor_one = jnp.exp(top_one - top_new)
    factor_two = jnp.exp(top_two - top_new)
    return (
        top_new,
        total_one * factor_one + total_two * factor_two,
        pooled_one * factor_one[..., None] + pooled_two * factor_two[..., None],
    )


PAIR = 2 * HEAD_DIM
SCALE = HEAD_DIM ** (-0.5)
HALF_TAPS = CONV_TAPS // 2


def dot_on(a, b, dim_a, dim_b):
    return lax.dot_general(
        a, b, (((dim_a,), (dim_b,)), ((), ())), preferred_element_type=jnp.float32
    )


def split_low(wide):
    high = wide.astype(jnp.bfloat16)
    return high, (wide - high.astype(jnp.float32)).astype(jnp.bfloat16)


def second_half(shape, dim):
    return lax.broadcasted_iota(jnp.int32, shape, dim) >= HEAD_DIM


def same_head(shape=(PAIR, PAIR)):
    return second_half(shape, 0) == second_half(shape, 1)


def pair_rows(block):
    wide = block.astype(jnp.float32)
    both = jnp.concatenate([wide, wide], axis=0)
    return jnp.where(same_head(), both, 0.0).astype(block.dtype)


def by_half(values, combine, neutral):
    late = second_half(values.shape, 1)
    first = combine(jnp.where(late, neutral, values), axis=1, keepdims=True)
    last = combine(jnp.where(late, values, neutral), axis=1, keepdims=True)
    return jnp.where(late, last, first)


def first_softmax(query, key_marks):
    scores = dot_on(query, key_marks, 1, 1) * SCALE
    powers = jnp.exp(scores - by_half(scores, jnp.max, -jnp.inf))
    return powers / by_half(powers, jnp.sum, 0.0)


def banded(toeplitz_ref, rim_ref, tokens):
    rows = toeplitz_ref.shape[1]
    columns = toeplitz_ref.shape[2]
    bands = []
    for start in range(0, tokens, rows):
        window = rim_ref[start : start + columns, :]
        first = dot_on(toeplitz_ref[0], window, 1, 0)
        last = dot_on(toeplitz_ref[1], window, 1, 0)
        bands.append(jnp.where(second_half(first.shape, 1), last, first))
    return jnp.concatenate(bands, axis=0) if len(bands) > 1 else bands[0]


def pool_kernel(key_ref, value_ref, ql_ref, pooled_ref):
    scores = dot_on(pair_rows(ql_ref[...]), key_ref[...], 1, 1) * SCALE
    top = jnp.max(scores, axis=1, keepdims=True)
    powers = jnp.exp(scores - top)
    total = jnp.sum(powers, axis=1, keepdims=True)
    high, low = split_low(powers)
    pooled = dot_on(high, value_ref[...], 1, 0) + dot_on(low, value_ref[...], 1, 0)
    pooled_ref[0, :, :PAIR] = jnp.where(same_head(), pooled, 0.0)
    late = second_half((PAIR, PAIR), 1)
    pooled_ref[0, :, PAIR:] = jnp.where(late, jnp.broadcast_to(total, late.shape), top)


def attend_kernel(query_ref, rim_ref, kl_ref, mixer_ref, toeplitz_ref, attended_ref):
    kernel = first_softmax(query_ref[...], pair_rows(kl_ref[...])).astype(jnp.bfloat16)
    mixed = dot_on(kernel, mixer_ref[0], 1, 0)
    tokens = query_ref.shape[0]
    attended_ref[...] = (mixed + banded(toeplitz_ref, rim_ref, tokens)).astype(jnp.bfloat16)


def query_back_kernel(
    query_ref, grad_ref, kl_ref, mixer_ref, sums_ref, query_grad_ref
):
    key_marks = pair_rows(kl_ref[...])
    kernel = first_softmax(query_ref[...], key_marks)
    mixer_part = dot_on(kernel.astype(jnp.bfloat16), grad_ref[...], 0, 0)
    sums_ref[0, :PAIR] = jnp.where(same_head(), mixer_part, 0.0)
    kern_grad = dot_on(grad_ref[...], mixer_ref[0], 1, 1)
    score_grad = kernel * (kern_grad - by_half(kernel * kern_grad, jnp.sum, 0.0))
    score_low = score_grad.astype(jnp.bfloat16)
    query_grad_ref[...] = dot_on(score_low, key_marks, 1, 0) * SCALE
    kl_part = dot_on(score_low, query_ref[...], 0, 0) * SCALE
    sums_ref[0, PAIR:] = jnp.where(same_head(), kl_part, 0.0)


def key_back_kernel(
    key_ref,
    value_ref,
    value_rim_ref,
    grad_ref,
    grad_rim_ref,
    ql_ref,
    pooled_grad_ref,
    means_ref,
    log_ref,
    toeplitz_ref,
    ql_part_ref,
    key_grad_ref,
    value_grad_ref,
    band_ref,
):
    query_marks = pair_rows(ql_ref[...])
    scores = dot_on(query_marks, key_ref[...], 1, 1) * SCALE
    kernel = jnp.exp(scores - log_ref[0][:, :1])
    grad_high, grad_low = split_low(pooled_grad_ref[0])
    kern_grad = dot_on(grad_high, value_ref[...], 1, 1) + dot_on(grad_low, value_ref[...], 1, 1)
    row_dot = jnp.sum(pooled_grad_ref[0] * means_ref[0], axis=1, keepdims=True)
    score_low = (kernel * (kern_grad - row_dot)).astype(jnp.bfloat16)
    ql_part = dot_on(score_low, key_ref[...], 1, 0) * SCALE
    ql_part_ref[0] = jnp.where(same_head(), ql_part, 0.0)
    key_grad_ref[...] = dot_on(score_low, query_marks, 0, 0) * SCALE
    kern_high, kern_low = split_low(kernel)
    value_grad = (
        dot_on(kern_high, grad_high, 0, 0)
        + dot_on(kern_high, grad_low, 0, 0)
        + dot_on(kern_low, grad_high, 0, 0)
    )
    tokens = key_ref.shape[0]
    rows, columns = toeplitz_ref.shape[1:]
    value_grad_ref[...] = (value_grad + banded(toeplitz_ref, grad_rim_ref, tokens)).astype(
        jnp.bfloat16
    )
    first = jnp.zeros((rows, columns), jnp.float32)
    last = first
    for start in range(0, tokens, rows):
        grads = grad_ref[start : start + rows, :]
        late = second_half(grads.shape, 1)
        window = value_rim_ref[start : start + columns, :]
        wide = grads.astype(jnp.float32)
        first = first + dot_on(jnp.where(late, 0.0, wide).astype(jnp.bfloat16), window, 1, 1)
        last = last + dot_on(jnp.where(late, wide, 0.0).astype(jnp.bfloat16), window, 1, 1)
    band_ref[0] = first
    band_ref[1] = last


def pair_call(body, operands, results):
    pairs = operands[0][0].shape[1] // PAIR

    def spec(kind, shape):
        if kind == "lanes":
            return pl.BlockSpec((shape[0], PAIR), lambda i: (0, i))
        if kind == "pair":
            return pl.BlockSpec((1,) + shape[1:], lambda i: (i, 0, 0))
        return pl.BlockSpec((2,) + shape[1:], lambda i: (i, 0, 0))

    flops = 2 * 12 * pairs * operands[0][0].shape[0] * PAIR * PAIR
    moved = 8 * sum(array.size for array, _ in operands)
    return pl.pallas_call(
        body,
        grid=(pairs,),
        in_specs=[spec(kind, array.shape) for array, kind in operands],
        out_specs=[spec(kind, shape) for shape, _, kind in results],
        out_shape=[jax.ShapeDtypeStruct(shape, dtype) for shape, dtype, _ in results],
        cost_estimate=pl.CostEstimate(flops=flops, bytes_accessed=moved, transcendentals=0),
    )(*[array for array, _ in operands])


def swap_sum(tree):
    if lax.axis_size("seq") == 2:
        other = jax.tree.map(lambda a: lax.ppermute(a, "seq", [(0, 1), (1, 0)]), tree)
        return jax.tree.map(lambda a, b: a + b, tree, other)
    return lax.psum(tree, "seq")


def swap_merge(part, combine):
    if lax.axis_size("seq") == 2:
        other = jax.tree.map(lambda a: lax.ppermute(a, "seq", [(0, 1), (1, 0)]), part)
        return combine(part, other)
    return combined_all(part, "seq", combine)


def to_documents(rows):
    blocks = lax.all_to_all(rows, "head", split_axis=0, concat_axis=0, tiled=True)
    return blocks.reshape(1, -1, rows.shape[2])


def to_positions(rows):
    blocks = rows.reshape(lax.axis_size("head"), -1, rows.shape[2])
    return lax.all_to_all(blocks, "head", split_axis=0, concat_axis=0, tiled=True)


def shifted(tree, axis, step):
    count = lax.axis_size(axis)
    links = [(i, (i + step) % count) for i in range(count)]
    return jax.tree.map(lambda a: lax.ppermute(a, axis, links), tree)


def block_before(axis, step):
    return lax.rem(lax.axis_index(axis) + lax.axis_size(axis) - step, lax.axis_size(axis))


def block_after(axis, step):
    return lax.rem(lax.axis_index(axis) + step, lax.axis_size(axis))


def own_share_rows(shard):
    rows, columns = shard.shape
    shares = lax.axis_size("row") * lax.axis_size("seq")
    place = lax.axis_index("row") * lax.axis_size("seq") + lax.axis_index("seq")
    return lax.dynamic_index_in_dim(shard.reshape(shares, rows // shares, columns), place, 0, False)


def gather_over_head(piece):
    return jnp.stack([shifted(piece, "head", k) for k in range(1, lax.axis_size("head"))])


def in_rows(values, columns):
    size = values.shape[-1]
    rows = -(-size // (16 * columns)) * 16
    pads = [(0, 0)] * (values.ndim - 1) + [(0, rows * columns - size)]
    return jnp.pad(values, pads).reshape(values.shape[:-1] + (rows, columns))


def gather_over_row(others):
    return [others] + [shifted(others, "row", k) for k in range(1, lax.axis_size("row"))]


def gather_over_seq(shards_here, shares):
    size_row, size_seq = lax.axis_size("row"), lax.axis_size("seq")
    shards = lax.axis_size("head")
    fulls = []
    for shard in shards_here:
        rows, columns = shard.shape
        parts = shard.reshape(1, size_row, size_seq, rows // (size_row * size_seq), columns)
        full = jnp.zeros((shards,) + parts.shape[1:], shard.dtype)
        fulls.append(lax.dynamic_update_slice(full, parts, (0, 0, 0, 0, 0)))
    for k in range(size_row):
        at_row = block_before("row", k)
        for j in range(size_seq):
            block = shares[k] if j == 0 else shifted(shares[k], "seq", j)
            start = 0
            for i, full in enumerate(fulls):
                part = block[:, start : start + full.shape[3]]
                start += full.shape[3]
                fulls[i] = lax.dynamic_update_slice(
                    full, part[:, None, None], (1, at_row, block_before("seq", j), 0, 0)
                )
    return [full.reshape(-1, full.shape[-1]) for full in fulls]


def sum_blocks(blocks, axis, dim):
    total = lax.dynamic_index_in_dim(blocks, lax.axis_index(axis), dim, False).astype(jnp.float32)
    for k in range(1, lax.axis_size(axis)):
        sent = lax.dynamic_index_in_dim(blocks, block_after(axis, k), dim, False)
        total = total + shifted(sent, axis, k).astype(jnp.float32)
    return total


def sum_shards(blocks):
    count = lax.axis_size("head")
    total = blocks[0].astype(jnp.float32)
    for k in range(1, count):
        total = total + shifted(blocks[k], "head", count - k).astype(jnp.float32)
    return total


def grads_over_seq(blocks):
    return sum_blocks(blocks, "seq", 1).astype(jnp.bfloat16)


def grads_over_row(low):
    return sum_blocks(low, "row", 0).astype(jnp.bfloat16)


def grads_over_head(low, shard_columns):
    shards = lax.axis_size("head")
    starts = [shards * sum(shard_columns[:i]) for i in range(len(shard_columns))]
    return sum_shards(
        [
            jnp.concatenate(
                [
                    low[:, start + k * width : start + (k + 1) * width]
                    for start, width in zip(starts, shard_columns)
                ],
                axis=1,
            )
            for k in range(shards)
        ]
    )


def norm_apply(residual, gain_row, shift_row):
    former = jnp.mean(residual, axis=-1)
    centered_raw = residual - former[..., None]
    variance = jnp.mean(centered_raw * centered_raw, axis=-1)
    inv_dev = lax.rsqrt(variance + EPS)
    centered = centered_raw * inv_dev[..., None]
    return (centered * gain_row + shift_row, centered, inv_dev)


def norm_back(incoming, centered, inv_dev, gain_row):
    scaled = incoming * gain_row
    former = jnp.mean(scaled, axis=-1)
    latter = jnp.mean(scaled * centered, axis=-1)
    return inv_dev[..., None] * (scaled - former[..., None] - centered * latter[..., None])


def norm_grads(incoming, centered):
    return jnp.stack([jnp.sum(incoming * centered, axis=(0, 1)), jnp.sum(incoming, axis=(0, 1))])


def on_device(
    inputs,
    segment_ids,
    w_project,
    proj_bias,
    conv_taps,
    w_output,
    out_bias,
    norm_attn,
    w_hidden,
    hid_bias,
    w_down,
    down_bias,
    norm_ffn,
    cotangent,
):
    model_width = inputs.shape[2]
    shards = lax.axis_size("head")
    heads_shard = w_project.shape[0]
    heads = heads_shard * shards
    hidden_shard = w_hidden.shape[1]
    width_shard = heads_shard * HEAD_DIM
    head_place = lax.axis_index("head")

    x_rows = to_documents(inputs)
    seqs, tokens, _ = x_rows.shape
    small_pack = jnp.concatenate([proj_bias.reshape(-1), conv_taps.reshape(-1), hid_bias])
    proj_rows = jnp.swapaxes(w_project, 0, 1).reshape(3 * width_shard, model_width)
    pin = lax.optimization_barrier
    first_shard = jnp.concatenate([proj_rows, w_output], axis=0)
    first_piece = own_share_rows(first_shard)
    share_rows = first_piece.shape[0]
    small_rows = in_rows(small_pack, model_width)
    first_shares = gather_over_head(jnp.concatenate([first_piece, small_rows], axis=0))
    small_all = jnp.concatenate([small_rows[None], first_shares[:, share_rows:]], axis=0)
    small_all = small_all.reshape(shards, -1)[:, : small_pack.shape[0]]
    first_shares = first_shares[:, :share_rows]
    later_shards, first_shares = pin(((w_hidden.T, w_down), first_shares))
    later_shares = gather_over_head(
        jnp.concatenate([own_share_rows(shard) for shard in later_shards], axis=0)
    )
    first_shares = gather_over_row(first_shares)
    proj_out = gather_over_seq([first_shard], first_shares)[0].reshape(shards, -1, model_width)
    split_one = 2 * width_shard
    split_two = split_one + heads_shard * CONV_TAPS
    bias_all = small_all[:, :split_one].reshape(shards, 2, width_shard)
    bias_all = jnp.swapaxes(bias_all, 0, 1).reshape(2, model_width)
    taps_all = small_all[:, split_one:split_two].reshape(heads, CONV_TAPS)
    hid_all = small_all[:, split_two:].reshape(shards * hidden_shard)

    proj_full = proj_out[:, : 3 * width_shard].reshape(shards, 3, width_shard, model_width)
    out_full = proj_out[:, 3 * width_shard :].reshape(model_width, model_width)
    grad_rows = to_documents(cotangent)

    segment_rows = lax.dynamic_slice_in_dim(segment_ids, head_place * seqs, seqs, axis=0)

    mixed_proj = [
        jnp.einsum(
            "ste,gfe->stgf", x_rows, proj_full[:, c], preferred_element_type=jnp.float32
        ).reshape(seqs, tokens, model_width)
        for c in range(3)
    ]
    query_tokens = (mixed_proj[0] + bias_all[0]).astype(jnp.bfloat16)
    key_tokens = mixed_proj[1].astype(jnp.bfloat16)
    value_tokens = (mixed_proj[2] + bias_all[1]).astype(jnp.bfloat16)
    query_tokens, later_shares = pin((query_tokens, later_shares))
    later_shares = gather_over_row(later_shares)
    segment_membership = (
        segment_rows[:, :, None] == jnp.arange(LANDMARKS, dtype=jnp.int32)[None, None, :]
    )
    member_low = segment_membership.astype(jnp.bfloat16)
    member_wide = segment_membership.astype(jnp.float32)
    query_sums = jnp.einsum(
        "stm,std->smd", member_low, query_tokens, preferred_element_type=jnp.float32
    )
    key_sums = jnp.einsum(
        "stm,std->smd", member_low, key_tokens, preferred_element_type=jnp.float32
    )
    segment_count = jnp.sum(member_wide, axis=1)
    count_lanes = jnp.broadcast_to(segment_count[..., None], segment_count.shape + (PAIR,))
    all_sums = swap_sum(jnp.concatenate([query_sums, key_sums, count_lanes], axis=-1))
    query_sums, key_sums = all_sums[..., :model_width], all_sums[..., model_width:-PAIR]
    segment_count = all_sums[..., -1]
    query_landmarks = (query_sums / segment_count[:, :, None]).astype(jnp.bfloat16)
    key_landmarks = (key_sums / segment_count[:, :, None]).astype(jnp.bfloat16)
    pairs = model_width // PAIR
    q_all, k_all, v_all = query_tokens[0], key_tokens[0], value_tokens[0]
    ql_all, kl_all = query_landmarks[0], key_landmarks[0]
    own_head = same_head()

    def paired(marks):
        blocks = jnp.swapaxes(marks.reshape(LANDMARKS, pairs, PAIR), 0, 1)
        both = jnp.concatenate([blocks, blocks], axis=1)
        return jnp.where(own_head, both, jnp.zeros_like(both))

    def unpaired(blocks):
        marks = blocks[:, :LANDMARKS] + blocks[:, LANDMARKS:]
        return jnp.swapaxes(marks, 0, 1).reshape(LANDMARKS, model_width)

    ql_pairs, kl_pairs = paired(ql_all), paired(kl_all)
    score_two = jnp.einsum("gmd,gnd->gmn", ql_pairs, kl_pairs, preferred_element_type=jnp.float32)
    score_two = jnp.where(own_head, score_two * SCALE, -jnp.inf)
    second_kernel = jax.nn.softmax(score_two, axis=-1)
    inverse, inverse_back = jax.vjp(newton_schulz_inverse, second_kernel)
    square = (pairs, PAIR, PAIR)
    pooled_local = pair_call(
        pool_kernel,
        [(k_all, "lanes"), (v_all, "lanes"), (ql_all, "lanes")],
        [((pairs, PAIR, 2 * PAIR), jnp.float32, "pair")],
    )[0]
    pooled_local, later_shares = pin((pooled_local, later_shares))
    hidden_full, down_full = gather_over_seq(later_shards, later_shares)

    def merge_pooled(former, latter):
        parts = [
            (part[:, :, PAIR], part[:, :, PAIR + HEAD_DIM], part[:, :, :PAIR])
            for part in (former, latter)
        ]
        top, total, pooled = merge_softmax(*parts)
        stats = [jnp.broadcast_to(a[..., None], a.shape + (HEAD_DIM,)) for a in (top, total)]
        return jnp.concatenate([pooled] + stats, axis=-1)

    merged = swap_merge(pooled_local, merge_pooled)
    pooled_all = merged[:, :, :PAIR]
    top_all, total_all = merged[:, :, PAIR], merged[:, :, PAIR + HEAD_DIM]
    segment_means = pooled_all / total_all[..., None]
    log_total = jnp.broadcast_to((top_all + jnp.log(total_all))[..., None], square)
    reduced_mixer = jnp.einsum(
        "gmn,gnd->gmd", inverse, segment_means, precision=HIGH_ACCURACY
    ).astype(jnp.bfloat16)
    value_rim = with_rims(value_tokens, HALF_TAPS)[0]
    band_rows = min(128, tokens)
    band_columns = band_rows + 2 * HALF_TAPS
    offsets = jnp.arange(band_columns)[None, :] - jnp.arange(band_rows)[:, None]
    tap_places = (offsets[None] == jnp.arange(CONV_TAPS)[:, None, None]).astype(jnp.bfloat16)
    toeplitz = jnp.einsum("hj,jpq->hpq", taps_all, tap_places)
    toeplitz_back = jnp.einsum("hj,jpq->hpq", taps_all[:, ::-1], tap_places)
    attended = pair_call(
        attend_kernel,
        [
            (q_all, "lanes"),
            (value_rim, "lanes"),
            (kl_all, "lanes"),
            (reduced_mixer, "pair"),
            (toeplitz, "heads"),
        ],
        [((tokens, model_width), jnp.bfloat16, "lanes")],
    )[0][None]
    out_part = jnp.dot(attended, out_full, preferred_element_type=jnp.float32)
    gain_one = norm_attn[0].astype(jnp.float32)
    shift_one = norm_attn[1].astype(jnp.float32)
    gain_two = norm_ffn[0].astype(jnp.float32)
    shift_two = norm_ffn[1].astype(jnp.float32)
    resid_one = x_rows.astype(jnp.float32) + out_part + out_bias.astype(jnp.float32)
    normed_one, centered_one, inv_one = norm_apply(resid_one, gain_one, shift_one)
    normed_low = normed_one.astype(jnp.bfloat16)
    hidden_pre = jnp.einsum(
        "ste,fe->stf", normed_low, hidden_full, preferred_element_type=jnp.float32
    ) + hid_all.astype(jnp.float32)
    active, gelu_back = jax.vjp(exact_gelu, hidden_pre)
    active_low = active.astype(jnp.bfloat16)
    down_part = jnp.dot(active_low, down_full, preferred_element_type=jnp.float32)
    resid_two = normed_one + down_part + down_bias.astype(jnp.float32)
    normed_two, centered_two, inv_two = norm_apply(resid_two, gain_two, shift_two)
    layer_out = to_positions(normed_two.astype(jnp.bfloat16))
    grad_y = grad_rows.astype(jnp.float32)
    grad_two = norm_back(grad_y, centered_two, inv_two, gain_two)
    norm_ffn_grad = norm_grads(grad_y, centered_two)
    down_low = grad_two.astype(jnp.bfloat16)
    down_bias_grad = jnp.sum(down_low, axis=(0, 1), dtype=jnp.float32)

    down_low, down_start = lax.optimization_barrier(
        (
            down_low,
            jnp.einsum(
                "stf,ste->ef", active_low, down_low, preferred_element_type=jnp.float32
            ).astype(jnp.bfloat16),
        )
    )
    grad_active = jnp.einsum("ste,fe->stf", down_low, down_full, preferred_element_type=jnp.float32)
    grad_pre = gelu_back(grad_active)[0].astype(jnp.bfloat16)
    hid_bias_grad = jnp.sum(grad_pre, axis=(0, 1), dtype=jnp.float32)
    grad_pre, hidden_start = lax.optimization_barrier(
        (
            grad_pre,
            jnp.einsum(
                "stf,ste->ef", grad_pre, normed_low, preferred_element_type=jnp.float32
            ).astype(jnp.bfloat16),
        )
    )
    back_part = jnp.einsum(
        "stf,fe->ste", grad_pre, hidden_full, preferred_element_type=jnp.float32
    )
    grad_in = grad_two + back_part
    grad_one = norm_back(grad_in, centered_one, inv_one, gain_one)
    norm_attn_grad = norm_grads(grad_in, centered_one)
    out_low = grad_one.astype(jnp.bfloat16)
    out_bias_grad = jnp.sum(out_low, axis=(0, 1), dtype=jnp.float32)
    out_low, out_start = lax.optimization_barrier(
        (
            out_low,
            jnp.einsum(
                "std,ste->ed", attended, out_low, preferred_element_type=jnp.float32
            ).astype(jnp.bfloat16),
        )
    )
    size_row, size_seq = lax.axis_size("row"), lax.axis_size("seq")

    def by_owner(grad):
        return grad.reshape(size_row, size_seq, model_width // (size_row * size_seq), -1)

    grad_att = jnp.einsum(
        "ste,de->std", out_low, out_full, preferred_element_type=jnp.float32
    ).astype(jnp.bfloat16)
    late_grads = grads_over_seq(
        jnp.concatenate([by_owner(g) for g in (down_start, hidden_start, out_start)], axis=3)
    )
    sums_part, query_grad = pair_call(
        query_back_kernel,
        [(q_all, "lanes"), (grad_att[0], "lanes"), (kl_all, "lanes"), (reduced_mixer, "pair")],
        [
            ((pairs, 2 * PAIR, PAIR), jnp.float32, "pair"),
            ((tokens, model_width), jnp.float32, "lanes"),
        ],
    )
    sums_part, late_grads = pin((sums_part, late_grads))
    late_grads = grads_over_row(late_grads)
    grad_rim = with_rims(grad_att, HALF_TAPS)[0]
    sums_all = swap_sum(sums_part)
    mixer_grad, kl_grad_one = sums_all[:, :PAIR], sums_all[:, PAIR:]
    inverse_grad = jnp.einsum("gmd,gnd->gmn", mixer_grad, segment_means, precision=HIGH_ACCURACY)
    pooled_grad = jnp.einsum("gmn,gmd->gnd", inverse, mixer_grad, precision=HIGH_ACCURACY)
    ql_part, key_grad, value_grad, band_sums = pair_call(
        key_back_kernel,
        [
            (k_all, "lanes"),
            (v_all, "lanes"),
            (value_rim, "lanes"),
            (grad_att[0], "lanes"),
            (grad_rim, "lanes"),
            (ql_all, "lanes"),
            (pooled_grad, "pair"),
            (segment_means, "pair"),
            (log_total, "pair"),
            (toeplitz_back, "heads"),
        ],
        [
            (square, jnp.float32, "pair"),
            ((tokens, model_width), jnp.float32, "lanes"),
            ((tokens, model_width), jnp.bfloat16, "lanes"),
            ((heads, band_rows, band_columns), jnp.float32, "heads"),
        ],
    )
    kern_two_grad = inverse_back(inverse_grad)[0]
    score_two_grad = second_kernel * (
        kern_two_grad - jnp.sum(second_kernel * kern_two_grad, axis=-1, keepdims=True)
    )
    ql_grad_two = jnp.einsum(
        "gmn,gnd->gmd", score_two_grad, kl_pairs.astype(jnp.float32), precision=HIGH_ACCURACY
    )
    kl_grad_two = jnp.einsum(
        "gmn,gmd->gnd", score_two_grad, ql_pairs.astype(jnp.float32), precision=HIGH_ACCURACY
    )
    ql_grad = unpaired(swap_sum(ql_part) + ql_grad_two * SCALE)
    kl_grad = unpaired(kl_grad_one + kl_grad_two * SCALE)
    per_count = 1.0 / segment_count[0][:, None]
    spreads = jnp.concatenate([ql_grad * per_count, kl_grad * per_count], axis=1)
    spread_high, spread_low = split_low(spreads)
    spread_rows = jnp.dot(
        member_low[0], spread_high, preferred_element_type=jnp.float32
    ) + jnp.dot(member_low[0], spread_low, preferred_element_type=jnp.float32)
    query_grad = query_grad + spread_rows[:, :model_width]
    key_grad = key_grad + spread_rows[:, model_width:]
    skewed = jnp.pad(band_sums.reshape(heads, band_rows * band_columns), ((0, 0), (0, band_rows)))
    taps_grad = jnp.sum(skewed.reshape(heads, band_rows, band_columns + 1), axis=1)[:, :CONV_TAPS]
    query_grad, key_grad, late_grads = pin((query_grad, key_grad, late_grads))
    late_grads = grads_over_head(late_grads, (hidden_shard, hidden_shard, width_shard))
    w_down_grad = late_grads[:, :hidden_shard]
    w_hidden_grad = late_grads[:, hidden_shard : 2 * hidden_shard]
    w_output_grad = late_grads[:, 2 * hidden_shard :]
    grads_qkv = jnp.stack(
        [
            part.astype(jnp.bfloat16).reshape(seqs, tokens, shards, width_shard)
            for part in (query_grad, key_grad, value_grad)
        ],
        axis=3,
    )
    proj_bias_grad = jnp.sum(grads_qkv[:, :, :, 0::2], axis=(0, 1), dtype=jnp.float32)
    proj_start = jnp.einsum(
        "str,ste->er", grads_qkv.reshape(seqs, tokens, -1), x_rows, preferred_element_type=jnp.float32
    ).astype(jnp.bfloat16)
    input_part = jnp.einsum(
        "stgcf,gcfe->ste", grads_qkv, proj_full, preferred_element_type=jnp.float32
    )
    input_grad = to_positions((input_part + grad_one).astype(jnp.bfloat16))

    def by_place(source):
        blocks = source.reshape(-1, shards, width_shard)
        return jnp.stack(
            [
                lax.dynamic_index_in_dim(blocks, block_before("head", k), 1, False).reshape(-1)
                for k in range(shards)
            ]
        )

    small_list = [
        proj_bias_grad.reshape(shards, -1),
        taps_grad.reshape(shards, -1),
        by_place(out_bias_grad),
        by_place(norm_attn_grad),
        hid_bias_grad.reshape(shards, -1),
        by_place(down_bias_grad),
        by_place(norm_ffn_grad),
    ]
    small_sum = in_rows(jnp.concatenate(small_list, axis=1), 3 * width_shard)
    small_sum = jnp.swapaxes(small_sum, 0, 1).reshape(small_sum.shape[1], -1).astype(jnp.bfloat16)
    small_blocks = jnp.broadcast_to(small_sum, (size_row, size_seq) + small_sum.shape)
    last_grads = grads_over_head(
        grads_over_row(
            grads_over_seq(jnp.concatenate([by_owner(proj_start), small_blocks], axis=2))
        ),
        (3 * width_shard,),
    )
    w_project_grad = last_grads[: -small_sum.shape[0]]
    small_sum = last_grads[-small_sum.shape[0] :].reshape(-1)
    outs, start_at = [], 0
    for part in small_list:
        outs.append(small_sum[start_at : start_at + part.shape[1]])
        start_at += part.shape[1]

    return (
        layer_out,
        input_grad,
        jnp.swapaxes(w_project_grad.T.reshape(3, heads_shard, HEAD_DIM, -1), 0, 1),
        outs[0].reshape(2, width_shard),
        outs[1].reshape(heads_shard, CONV_TAPS),
        w_output_grad.T,
        outs[2],
        outs[3].reshape(2, width_shard),
        w_hidden_grad,
        outs[4],
        w_down_grad.T,
        outs[5],
        outs[6].reshape(2, width_shard),
    )


def solution(mesh):
    in_specs = (
        P("row", ("seq", "head"), None),
        P("row", "seq"),
        P("head", None, None, None),
        P(None, "head"),
        P("head", None),
        P("head", None),
        P(),
        P(),
        P(None, "head"),
        P("head"),
        P("head", None),
        P(),
        P(),
        P("row", ("seq", "head"), None),
    )
    out_specs = (
        P("row", ("seq", "head"), None),
        P("row", ("seq", "head"), None),
        P("head", None, None, ("row", "seq")),
        P(None, "head"),
        P("head", None),
        P("head", ("row", "seq")),
        P("head"),
        P(None, "head"),
        P(("row", "seq"), "head"),
        P("head"),
        P("head", ("row", "seq")),
        P("head"),
        P(None, "head"),
    )
    return jax.shard_map(
        on_device, mesh=mesh, in_specs=in_specs, out_specs=out_specs, check_vma=False
    )
```
